128 devices in a mesh: gx: 16 (over z, x), gy: 8 (over y, core).
Axes of the slice: x: 4, y: 4, z: 4, core: 2. Of those that a mesh axis runs over, the one named last changes fastest.
Arguments:
- anchors: float32 [3, 4096], P(None, ('gx', 'gy')), may hold values from 0 to 1
- directions: float32 [3, 4096], P(None, ('gx', 'gy')), may hold values from -1 to 1
- ray_start: float32 [4096], P(('gx', 'gy')), may hold values from 0 to 1
- camera_ids: int32 [4096], P(('gx', 'gy')), may hold values from 0 to 255
- brick_ids: int32 [4096, 4], P(('gx', 'gy')), may hold values from 0 to 127, all different within a row; in each aligned block of 32 rows (0 to 31, 32 to 63, ...) at most 2 rows name the same one
- brick_rank: int32 [4096, 4], P(('gx', 'gy')), may hold values from 0 to 3, each once within a row
- targets: float32 [4096, 128], P(('gx', 'gy')), may hold values from -6 to 6
- planes: float32 [128, 12288, 128], P(('gx', 'gy')), may hold values from -6 to 6
- first_weight: float32 [128, 128, 256], P(('gx', 'gy')), may hold values from -0.5 to 0.5
- hidden_weight: float32 [128, 1, 256, 256], P(('gx', 'gy')), may hold values from -0.375 to 0.375
- feature_weight: float32 [128, 256, 128], P(('gx', 'gy')), may hold values from -0.375 to 0.375
- density_weight: float32 [128, 256], P(('gx', 'gy')), may hold values from -0.375 to 0.375
- poses: float32 [6, 256], replicated, may hold values from -0.1 to 0.1
Outputs:
- ray_feature: float32 [4096, 128], P(('gx', 'gy'))
- plane_grad: float32 [128, 12288, 128], P(('gx', 'gy'))
- first_grad: float32 [128, 128, 256], P(('gx', 'gy'))
- hidden_grad: float32 [128, 1, 256, 256], P(('gx', 'gy'))
- feature_grad: float32 [128, 256, 128], P(('gx', 'gy'))
- density_grad: float32 [128, 256], P(('gx', 'gy'))
- pose_grad: float32 [6, 256], replicated
The draws below stay inside these ranges and needn't reach their ends.
Inputs may be any that keep to these rules, and one draw needn't show every extreme that they name: `brick_ids`: each ray names 4 different bricks; among the rays of one device no brick is named more than 2 times, and in every draw some device's rays name some brick exactly 2 times. `brick_rank`: each row holds every number of 0 to 3 once.
All inputs are finite; a program needn't handle non-finite values.
Results may differ from the reference program's by a relative error of at most 0.014.
Values sent between devices are 32-bit elements; how exact they have to be, the bound alone decides.
No kernel may reach another device: no remote copies, remote signals or barrier semaphores. Data moves between devices by JAX's collectives and lax.ppermute only.
A program may use at most 256 MiB of HBM per device.

```python
import math
import jax
import jax.numpy as jnp
import numpy as np
from jax import lax

C = 128
H = 256
DEPTH = 2
K = 4
S = 4
P_SIZE = 64
NCAM = 256
RAYS_DEV = 32
BRICKS = 128
CAP = 2
RAYS = 4096


def set_ends(values, rng, least, high):
    longest = values.shape.index(max(values.shape))
    spots = []
    for shift in (0, 1):
        where = [jax.random.randint(jax.random.fold_in(rng, axis), (), 0, length) for axis, length in enumerate(values.shape)]
        where[longest] = (where[longest] + shift) % values.shape[longest]
        spots.append(tuple(where))
    return values.at[spots[0]].set(least).at[spots[1]].set(high)


def level_of(rng, dims, cuts, least, largest):
    loudness = 1.0
    for dim, blocks in cuts:
        heights = jax.random.uniform(jax.random.fold_in(jax.random.fold_in(rng, 6), dim), (blocks,), jnp.float32, least / len(cuts), largest / len(cuts))
        loudness = loudness * jnp.repeat(jnp.exp(heights), dims[dim] // blocks).reshape((-1,) + (1,) * (len(dims) - 1 - dim))
    return loudness


def shared_out(key, own, number, rows, number_of, top, bound, skew):
    order = jax.random.permutation(key, number_of)
    crowded, common = shares(number_of, rows * top, bound, skew, True), shares(number_of, rows * top, bound, skew, False)
    places = jnp.arange(number_of)

    def named(lengths, turn):
        used = int((lengths > 0).sum())
        fixed = max(1, used // 4)
        moved = fixed + (places - fixed + turn * (used - fixed)) % max(1, number_of - fixed)
        return jnp.zeros((number_of,), jnp.int32).at[order[jnp.where(places < fixed, places, moved)]].set(jnp.asarray(lengths, jnp.int32))

    lengths = jnp.where(number % 4 == 0, named(crowded, number // 4), named(common, number - number // 4 - 1))
    mixed = jax.random.permutation(jax.random.fold_in(own, 3), number_of)
    source_of, sink = mixed[0:number_of // 2 * 2:2], mixed[1:number_of // 2 * 2:2]
    slack = jnp.minimum(lengths[source_of] - 1, bound - lengths[sink]) // 2
    slack = jnp.where((source_of == order[0]) | (sink == order[0]) | (lengths[sink] == 0), 0, jnp.maximum(slack, 0))
    moved = jax.random.randint(jax.random.fold_in(own, 4), (number_of // 2,), 0, 1 << 20) % (slack + 1)
    lengths = lengths.at[source_of].add(-moved).at[sink].add(moved)
    members = jnp.searchsorted(jnp.cumsum(lengths), jnp.arange(rows * top), side="right").astype(jnp.int32)
    table = members.reshape(top, rows).T
    table = table[jax.random.permutation(jax.random.fold_in(own, 1), rows)]
    turn = jax.random.randint(jax.random.fold_in(own, 2), (rows, 1), 0, top)
    return jnp.take_along_axis(table, (jnp.arange(top)[None, :] + turn) % top, axis=1)


def shares(count, total, bound, slope, full):
    loads = [(1 << 20) // math.isqrt(grade ** slope) + 1 for grade in range(1, count + 1)]
    largest = bound if full else min(bound, max(-(-total // count), total * loads[0] // sum(loads)))
    least = 1 if total - largest >= count - 1 else 0
    counts, spare = [largest] + [least] * (count - 1), total - largest - least * (count - 1)
    while spare > 0:
        free = [i for i in range(1, count) if counts[i] < largest] or [i for i in range(1, count) if counts[i] < bound]
        mass, remaining = sum([loads[i] for i in free]), spare
        for i in free:
            addition = min(bound - counts[i], max(1, remaining * loads[i] // mass), spare)
            counts[i] = counts[i] + addition
            spare = spare - addition
    return np.array(counts)


def normal_values(own_key, shape, width, limit, split=(), kind=jnp.bfloat16):
    drawn = width * jax.random.normal(own_key, shape, jnp.float32)
    if split:
        drawn = drawn * level_of(own_key, shape, split, -0.22, 0.18)
    return jnp.clip(drawn, -limit, limit).astype(kind)


def setup_inputs(seed: int = 0) -> dict:
    key_of = jax.random.split(jax.random.key(seed), 14)
    anchors = jnp.clip(1.0 * jax.random.uniform(key_of[0], (3, RAYS), jnp.float32) ** level_of(key_of[0], (3, RAYS), ((1, 128),), -0.2, 0.2), 0.0, 1.0)
    directions = jnp.clip(jax.random.uniform(key_of[1], (3, RAYS), jnp.float32, -1.0, 1.0) * level_of(key_of[1], (3, RAYS), ((1, 128),), -0.4, 0.0), -1.0, 1.0)
    ray_start = jnp.clip(1.0 * jax.random.uniform(key_of[2], (RAYS,), jnp.float32) ** level_of(key_of[2], (RAYS,), ((0, 128),), -0.2, 0.2), 0.0, 1.0)
    camera_ids = set_ends(jax.random.randint(key_of[3], (RAYS,), 0, NCAM), jax.random.fold_in(key_of[3], 1), 0, NCAM - 1).astype(jnp.int32)
    brick_ids_keys = jax.random.split(jax.random.fold_in(key_of[4], 1), RAYS // RAYS_DEV)
    brick_ids_turns = jax.random.permutation(jax.random.fold_in(key_of[4], 3), RAYS // RAYS_DEV)
    brick_ids = jax.vmap(lambda own, number: shared_out(jax.random.fold_in(key_of[4], 2), own, number, RAYS_DEV, BRICKS, K, CAP, 2))(brick_ids_keys, brick_ids_turns).reshape((RAYS, K))
    brick_rank = jax.vmap(lambda own: jax.random.permutation(own, K))(jax.random.split(key_of[5], RAYS)).reshape((RAYS, K)).astype(jnp.int32)
    targets = normal_values(key_of[6], (RAYS, C), 1.0, 6.0, ((0, 128),), jnp.float32)
    planes = normal_values(key_of[7], (BRICKS, 3 * P_SIZE * P_SIZE, C), 1.0, 6.0, ((0, 128),), jnp.float32)
    first_weight = normal_values(key_of[8], (BRICKS, C, H), C ** -0.5, 0.5, ((0, 128),), jnp.float32)
    hidden_weight = normal_values(key_of[9], (BRICKS, DEPTH - 1, H, H), H ** -0.5, 0.375, ((0, 128),), jnp.float32)
    feature_weight = normal_values(key_of[10], (BRICKS, H, C), H ** -0.5, 0.375, ((0, 128),), jnp.float32)
    density_weight = normal_values(key_of[11], (BRICKS, H), H ** -0.5, 0.375, ((0, 128),), jnp.float32)
    poses = jnp.clip(jax.random.uniform(key_of[12], (6, NCAM), jnp.float32, -0.1, 0.1), -0.1, 0.1)
    return {"anchors": anchors, "directions": directions, "ray_start": ray_start, "camera_ids": camera_ids, "brick_ids": brick_ids, "brick_rank": brick_rank, "targets": targets, "planes": planes, "first_weight": first_weight, "hidden_weight": hidden_weight, "feature_weight": feature_weight, "density_weight": density_weight, "poses": poses}


sample_step = 0.125
plane_pairs = ((0, 1), (0, 2), (1, 2))

def smooth_weight(fraction):
    return fraction * fraction * (3.0 - 2.0 * fraction)

def lookup(planes_flat, points):
    summed = jnp.zeros((points.shape[1], planes_flat.shape[1]), jnp.float32)
    for plane_index, coord_pair in enumerate(plane_pairs):
        coord_u = points[coord_pair[0]] * P_SIZE
        coord_v = points[coord_pair[1]] * P_SIZE
        floor_u = jnp.floor(coord_u)
        floor_v = jnp.floor(coord_v)
        weight_u = smooth_weight(coord_u - floor_u)[:, None]
        weight_v = smooth_weight(coord_v - floor_v)[:, None]
        low_u = jnp.mod(floor_u.astype(jnp.int32), P_SIZE)
        low_v = jnp.mod(floor_v.astype(jnp.int32), P_SIZE)
        high_u = jnp.mod(low_u + 1, P_SIZE)
        high_v = jnp.mod(low_v + 1, P_SIZE)
        plane_base = plane_index * P_SIZE * P_SIZE
        corner_aa = planes_flat[plane_base + low_u * P_SIZE + low_v]
        corner_ab = planes_flat[plane_base + low_u * P_SIZE + high_v]
        corner_ba = planes_flat[plane_base + high_u * P_SIZE + low_v]
        corner_bb = planes_flat[plane_base + high_u * P_SIZE + high_v]
        summed = summed + (1.0 - weight_u) * ((1.0 - weight_v) * corner_aa + weight_v * corner_ab) + weight_u * ((1.0 - weight_v) * corner_ba + weight_v * corner_bb)
    return summed

def brick_samples(planes_flat, first_weight, hidden_weight, feature_weight, density_weight, received):
    sources, slot_total, flat_width = received.shape
    points = received.reshape(sources * slot_total, 3, S).transpose(1, 0, 2).reshape(3, -1)
    features = lookup(planes_flat, points).astype(jnp.bfloat16)
    hidden = jax.nn.silu(jnp.dot(features, first_weight.astype(jnp.bfloat16), preferred_element_type=jnp.float32)).astype(jnp.bfloat16)
    for layer_index in range(hidden_weight.shape[0]):
        hidden = jax.nn.silu(jnp.dot(hidden, hidden_weight[layer_index].astype(jnp.bfloat16), preferred_element_type=jnp.float32)).astype(jnp.bfloat16)
    colors = jnp.tanh(jnp.dot(hidden, feature_weight.astype(jnp.bfloat16), preferred_element_type=jnp.float32))
    density = jax.nn.softplus(jnp.dot(hidden, density_weight.astype(jnp.bfloat16), preferred_element_type=jnp.float32))
    return (colors.reshape(sources, slot_total, -1), density.reshape(sources, slot_total, S))

def composite(density, colors):
    optical_depth = density * sample_step
    before = jnp.cumsum(optical_depth, axis=-1) - optical_depth
    weight = jnp.exp(-before) * (1.0 - jnp.exp(-optical_depth))
    feature = lax.optimization_barrier(jnp.sum(weight[..., None] * colors, axis=-2))
    passing = jnp.exp(-lax.optimization_barrier(jnp.sum(optical_depth, axis=-1)))
    return (feature, passing)

def brick_segments(planes_flat, first_weight, hidden_weight, feature_weight, density_weight, received):
    colors, density = brick_samples(planes_flat, first_weight, hidden_weight, feature_weight, density_weight, received)
    sources, slot_total, flat_width = colors.shape
    return composite(density, colors.reshape(sources, slot_total, S, -1))

def ray_composite(segment_feature, segment_pass, brick_rank):
    transmit = jnp.ones(segment_pass.shape, segment_pass.dtype)
    for other_seg in range(K):
        in_front = brick_rank[:, other_seg][:, None] < brick_rank
        transmit = transmit * jnp.where(in_front, segment_pass[:, other_seg][:, None], 1.0)
    return lax.optimization_barrier(jnp.sum(transmit[:, :, None] * segment_feature, axis=1))

def cross_rows(left, right):
    return jnp.stack([left[1] * right[2] - left[2] * right[1], left[2] * right[0] - left[0] * right[2], left[0] * right[1] - left[1] * right[0]])

def sample_points(anchors, directions, ray_start, ray_pose, brick_rank):
    rotation = ray_pose[0:3]
    offset = ray_pose[3:6]
    moved_anchor = anchors + cross_rows(rotation, anchors) + offset
    moved_direction = directions + cross_rows(rotation, directions)
    place_along = brick_rank.astype(jnp.float32)[:, :, None] * S + jnp.arange(S)[None, None, :] + 0.5
    distance = ray_start[:, None, None] + place_along * sample_step
    return moved_anchor[:, :, None, None] + distance[None] * moved_direction[:, :, None, None]

def slot_numbers(target_brick, brick_count):
    onehot = (target_brick[:, None] == jnp.arange(brick_count)[None, :]).astype(jnp.int32)
    before = jnp.cumsum(onehot, axis=0) - onehot
    return lax.optimization_barrier(jnp.sum(before * onehot, axis=1)).astype(jnp.int32)

def reference(anchors, directions, ray_start, camera_ids, brick_ids, brick_rank, targets, planes, first_weight, hidden_weight, feature_weight, density_weight, poses):
    ray_count = anchors.shape[1]
    per_device = ray_count // BRICKS
    selector = (jnp.arange(NCAM)[:, None] == camera_ids[None, :]).astype(jnp.float32)

    def place(pose_table):
        ray_pose = jnp.dot(pose_table, selector, precision=lax.Precision.HIGHEST)
        return sample_points(anchors, directions, ray_start, ray_pose, brick_rank)
    points, pose_pullback = jax.vjp(place, poses)
    payload = points.transpose(1, 2, 0, 3).reshape(ray_count * K, 3 * S)
    target_brick = brick_ids.reshape(BRICKS, per_device * K).astype(jnp.int32)

    def per_row(row_bricks):
        return slot_numbers(row_bricks, BRICKS)
    slot_table = jax.vmap(per_row)(target_brick)
    source_dev = jnp.arange(BRICKS).astype(jnp.int32)[:, None]
    flat_slot = (target_brick * (BRICKS * CAP) + source_dev * CAP + slot_table).reshape(-1).astype(jnp.int32)
    incoming = jnp.zeros((BRICKS * BRICKS * CAP, 3 * S), jnp.float32).at[flat_slot].set(payload)
    incoming = incoming.reshape(BRICKS, BRICKS, CAP, 3 * S)
    stacked = (planes, first_weight, hidden_weight, feature_weight, density_weight)

    def forward_one(pieces):
        return brick_segments(pieces[0], pieces[1], pieces[2], pieces[3], pieces[4], pieces[5])
    seg_values, seg_optical = lax.map(forward_one, stacked + (incoming,))
    segment_values = seg_values.reshape(-1, C)[flat_slot]
    segment_optical = seg_optical.reshape(-1)[flat_slot]

    def ray_from(values_part, optical_part):
        return ray_composite(values_part.reshape(ray_count, K, C), optical_part.reshape(ray_count, K), brick_rank)
    ray_feature, ray_pullback = jax.vjp(ray_from, segment_values, segment_optical)
    values_grad, optical_grad = ray_pullback(ray_feature - targets)
    values_back = jnp.zeros((BRICKS * BRICKS * CAP, C), jnp.float32).at[flat_slot].set(values_grad).reshape(BRICKS, BRICKS, CAP, C)
    optical_back = jnp.zeros((BRICKS * BRICKS * CAP,), jnp.float32).at[flat_slot].set(optical_grad).reshape(BRICKS, BRICKS, CAP)

    def backward_one(pieces):
        outputs_unused, pullback = jax.vjp(brick_segments, pieces[0], pieces[1], pieces[2], pieces[3], pieces[4], pieces[5])
        return pullback((pieces[6], pieces[7]))
    gradients = lax.map(backward_one, stacked + (incoming, values_back, optical_back))
    point_grad = gradients[5].reshape(-1, 3 * S)[flat_slot].reshape(ray_count, K, 3, S).transpose(2, 0, 1, 3)
    pose_grad = pose_pullback(point_grad)[0]
    return (ray_feature, gradients[0], gradients[1], gradients[2], gradients[3], gradients[4], pose_grad)
```

```python
import jax
import jax.numpy as jnp
from jax import lax
from jax.experimental import pallas as pl
from jax.experimental.pallas import tpu as pltpu
from jax.sharding import PartitionSpec as P

K = 4
S = 4
CELLS = 64
LANES = 128
STEP = 0.125
AXES = ("gx", "gy")
F32 = jnp.float32
BF16 = jnp.bfloat16
EXACT = lax.Precision.HIGHEST


def contract(left, right, left_dim, right_dim, precision=None):
    return lax.dot_general(
        left,
        right,
        (((left_dim,), (right_dim,)), ((), ())),
        precision=precision,
        preferred_element_type=F32,
    )


def iota(shape, dim):
    return lax.broadcasted_iota(jnp.int32, shape, dim)


def eye(size):
    return (iota((size, size), 0) == iota((size, size), 1)).astype(F32)


def dispatch_kernel(anchors, directions, start, cameras, ids, ranks, out, route, packed):
    rays = anchors.shape[1]
    segs = rays * K
    bricks = route.shape[0] // 2
    spread = (iota((rays, segs), 0) == iota((rays, segs), 1) % rays).astype(F32)
    own = iota((K, segs), 0) == iota((K, segs), 1) // rays
    id4 = contract(ids[...].astype(F32), spread, 0, 0, EXACT)
    id_row = jnp.sum(jnp.where(own, id4, 0.0), axis=0, keepdims=True)
    rank4 = contract(ranks[...].astype(F32), spread, 0, 0, EXACT)
    rank_row = jnp.sum(jnp.where(own, rank4, 0.0), axis=0, keepdims=True)
    packed[0:3, :] = contract(anchors[...], spread, 1, 0, EXACT)
    packed[3:6, :] = contract(directions[...], spread, 1, 0, EXACT)
    packed[6:7, :] = contract(start[...], spread, 1, 0, EXACT) + rank_row * (S * STEP)
    packed[7:8, :] = contract(cameras[...].astype(F32), spread, 1, 0, EXACT)
    onehot = (iota((bricks, segs), 0) == id_row.astype(jnp.int32)).astype(F32)
    earlier = (iota((segs, segs), 0) < iota((segs, segs), 1)).astype(F32)
    before = contract(onehot, earlier, 1, 0)
    for slot in range(2):
        taken = jnp.where((before > 0.5) == (slot == 1), onehot, 0.0)
        route[slot * bricks : (slot + 1) * bricks, :] = taken
        rows = contract(taken, packed[...], 1, 1, EXACT)
        out[:, slot * LANES : slot * LANES + 8] = rows


def dispatch(anchors, directions, start, cameras, ids, ranks, bricks):
    rays = anchors.shape[1]
    return pl.pallas_call(
        dispatch_kernel,
        out_shape=(
            jax.ShapeDtypeStruct((bricks, 2 * LANES), F32),
            jax.ShapeDtypeStruct((2 * bricks, rays * K), F32),
        ),
        scratch_shapes=[pltpu.VMEM((8, rays * K), F32)],
        name="dispatch",
    )(anchors, directions, start, cameras, ids, ranks)


def ray_rows(received, poses, sources):
    cols = contract(received[...], eye(sources), 0, 0, EXACT)
    rows = jnp.concatenate([cols[0:8], cols[LANES : LANES + 8]], axis=1)
    slots = 2 * sources
    cams = poses.shape[1]
    picked = (iota((cams, slots), 0) == rows[7:8].astype(jnp.int32)).astype(F32)
    pose = contract(poses[...], picked, 1, 0, EXACT)
    return rows, picked, pose


def cross(a, b):
    return (
        a[1] * b[2] - a[2] * b[1],
        a[2] * b[0] - a[0] * b[2],
        a[0] * b[1] - a[1] * b[0],
    )


def sample_rows(rows, pose):
    anchor = [rows[i : i + 1] for i in range(3)]
    direction = [rows[3 + i : 4 + i] for i in range(3)]
    turn = [pose[i : i + 1] for i in range(3)]
    shift = [pose[3 + i : 4 + i] for i in range(3)]
    turned = cross(turn, anchor)
    moved = [anchor[i] + turned[i] + shift[i] for i in range(3)]
    bent = cross(turn, direction)
    heading = [direction[i] + bent[i] for i in range(3)]
    distance = [rows[6:7] + (s + 0.5) * STEP for s in range(S)]
    return [
        jnp.concatenate([moved[i] + distance[s] * heading[i] for s in range(S)], axis=1)
        for i in range(3)
    ]


def factors(coordinate):
    count = coordinate.shape[1]
    scaled = coordinate * CELLS
    floor_c = jnp.floor(scaled)
    fraction = scaled - floor_c
    weight = fraction * fraction * (3.0 - 2.0 * fraction)
    slope = (6.0 * CELLS) * fraction * (1.0 - fraction)
    low = lax.bitwise_and(floor_c.astype(jnp.int32), CELLS - 1)
    high = lax.bitwise_and(low + 1, CELLS - 1)
    cell = iota((CELLS, count), 0)
    at_low = cell == low
    at_high = cell == high
    value = jnp.where(at_low, 1.0 - weight, 0.0) + jnp.where(at_high, weight, 0.0)
    change = jnp.where(at_high, slope, 0.0) - jnp.where(at_low, slope, 0.0)
    return value, change


BLOCK = 1024
TILE = 256


def plane_axes(step):
    plane = step // (CELLS * CELLS // BLOCK)
    first = plane // 2
    second = jnp.minimum(plane + 1, 2)
    start = (step % (CELLS * CELLS // BLOCK)) * (BLOCK // CELLS)
    return first * CELLS + start, second * CELLS, first, second


def table_tile(rows_ref, row_base, part, columns, lane):
    pieces = []
    for i in range(TILE // CELLS):
        row = rows_ref[pl.ds(row_base + part * (TILE // CELLS) + i, 1), lane : lane + TILE]
        pieces.append((row * columns).astype(BF16))
    return jnp.concatenate(pieces, axis=0)


def forward_kernel(
    received, poses, planes, first_w, hidden_w, feature_w, density_w,
    out, rows_out, pose_out, factor_out, slope_out, feats_out, v1_out, v2_out, colors_out, dens_out,
    total, turned,
):
    step = pl.program_id(0)
    sources = received.shape[0]
    count = 2 * sources * S

    @pl.when(step == 0)
    def _():
        rows, _, pose = ray_rows(received, poses, sources)
        rows_out[...] = rows
        pose_out[...] = jnp.concatenate([pose, pose[0:2]], axis=0)
        for axis, coordinate in enumerate(sample_rows(rows, pose)):
            value, change = factors(coordinate)
            factor_out[axis * CELLS : (axis + 1) * CELLS, :] = value
            slope_out[axis * CELLS : (axis + 1) * CELLS, :] = change
        total[...] = jnp.zeros_like(total)

    row_base, col_base, _, _ = plane_axes(step)
    turned[...] = planes[...].T.astype(BF16)
    for lane in range(0, count, TILE):
        columns = factor_out[pl.ds(pl.multiple_of(col_base, CELLS), CELLS), lane : lane + TILE]
        acc = total[:, lane : lane + TILE]
        for part in range(BLOCK // TILE):
            tile = table_tile(factor_out, row_base, part, columns, lane)
            acc = acc + contract(turned[:, part * TILE : (part + 1) * TILE], tile, 1, 0)
        total[:, lane : lane + TILE] = acc

    @pl.when(step == pl.num_programs(0) - 1)
    def _():
        slots = 2 * sources
        feats = total[...].astype(BF16)
        feats_out[...] = feats
        v1 = contract(first_w[...].T.astype(BF16), feats, 1, 0)
        v1_out[...] = v1
        h1 = (v1 * jax.nn.sigmoid(v1)).astype(BF16)
        v2 = contract(hidden_w[...].T.astype(BF16), h1, 1, 0)
        v2_out[...] = v2
        h2 = (v2 * jax.nn.sigmoid(v2)).astype(BF16)
        colors = jnp.tanh(contract(feature_w[...].T.astype(BF16), h2, 1, 0))
        colors_out[...] = colors
        raw = contract(density_w[...].astype(BF16), h2, 1, 0)
        dens_out[...] = raw
        depth = (jnp.maximum(raw, 0.0) + jnp.log1p(jnp.exp(-jnp.abs(raw)))) * STEP
        seg = jnp.zeros((LANES, slots), F32)
        front = jnp.zeros((1, slots), F32)
        for s in range(S):
            e = depth[:, s * slots : (s + 1) * slots]
            weight = jnp.exp(-front) * (1.0 - jnp.exp(-e))
            seg = seg + weight * colors[:, s * slots : (s + 1) * slots]
            front = front + e
        through = jnp.exp(-front)
        out[:, 0:LANES] = seg[:, 0:sources].T
        out[:, LANES : 2 * LANES] = seg[:, sources:slots].T
        sub = iota((8, sources), 0)
        both = jnp.where(
            sub == 0, through[:, 0:sources], jnp.where(sub == 1, through[:, sources:slots], 0.0)
        )
        place = (iota((8, LANES), 0) == iota((8, LANES), 1)).astype(F32)
        out[:, 2 * LANES : 3 * LANES] = contract(both, place, 0, 0, EXACT)


def whole(shape):
    return pl.BlockSpec(shape, lambda step: (0,) * len(shape))


def forward(received, poses, planes, first_w, hidden_w, feature_w, density_w):
    sources = received.shape[0]
    slots = 2 * sources
    count = slots * S
    channels = planes.shape[1]
    hidden = first_w.shape[1]
    outs = [
        ((sources, 3 * LANES), F32),
        ((8, slots), F32),
        ((8, slots), F32),
        ((3 * CELLS, count), F32),
        ((3 * CELLS, count), F32),
        ((channels, count), BF16),
        ((hidden, count), F32),
        ((hidden, count), F32),
        ((channels, count), F32),
        ((1, count), F32),
    ]
    ins = [received, poses, planes, first_w, hidden_w, feature_w, density_w]
    specs = [whole(x.shape) for x in ins]
    specs[2] = pl.BlockSpec((BLOCK, channels), lambda step: (step, 0))
    return pl.pallas_call(
        forward_kernel,
        grid=(planes.shape[0] // BLOCK,),
        in_specs=specs,
        out_specs=[whole(shape) for shape, _ in outs],
        out_shape=[jax.ShapeDtypeStruct(shape, kind) for shape, kind in outs],
        scratch_shapes=[pltpu.VMEM((channels, count), F32), pltpu.VMEM((channels, BLOCK), BF16)],
        compiler_params=pltpu.CompilerParams(vmem_limit_bytes=40 * 2**20),
        name="forward",
    )(*ins)


def slope_kernel(factor, slope, planes, out, turned):
    step = pl.program_id(0)
    count = factor.shape[1]

    @pl.when(step == 0)
    def _():
        out[...] = jnp.zeros_like(out)

    row_base, col_base, first, second = plane_axes(step)
    turned[...] = planes[...].T.astype(BF16)
    for rows_ref, cols_ref, axis in ((slope, factor, first), (factor, slope, second)):
        base = pl.multiple_of(axis * LANES, LANES)
        for lane in range(0, count, TILE):
            columns = cols_ref[pl.ds(pl.multiple_of(col_base, CELLS), CELLS), lane : lane + TILE]
            acc = out[pl.ds(base, LANES), lane : lane + TILE]
            for part in range(BLOCK // TILE):
                tile = table_tile(rows_ref, row_base, part, columns, lane)
                acc = acc + contract(turned[:, part * TILE : (part + 1) * TILE], tile, 1, 0)
            out[pl.ds(base, LANES), lane : lane + TILE] = acc


def slopes(factor, slope, planes):
    count = factor.shape[1]
    channels = planes.shape[1]
    return pl.pallas_call(
        slope_kernel,
        grid=(planes.shape[0] // BLOCK,),
        in_specs=[
            whole(factor.shape),
            whole(slope.shape),
            pl.BlockSpec((BLOCK, channels), lambda step: (step, 0)),
        ],
        out_specs=whole((3 * channels, count)),
        out_shape=jax.ShapeDtypeStruct((3 * channels, count), F32),
        scratch_shapes=[pltpu.VMEM((channels, BLOCK), BF16)],
        compiler_params=pltpu.CompilerParams(vmem_limit_bytes=40 * 2**20),
        name="slopes",
    )(factor, slope, planes)


def rays_kernel(home, route, ranks, targets, ray_out, back, grads):
    bricks = home.shape[0]
    rays = targets.shape[0]
    slot = [route[0:bricks, :].T, route[bricks : 2 * bricks, :].T]
    seg = contract(slot[0], home[:, 0:LANES], 1, 0, EXACT) + contract(
        slot[1], home[:, LANES : 2 * LANES], 1, 0, EXACT
    )
    lane = iota((1, LANES), 1)
    through = home[:, 2 * LANES : 3 * LANES]
    passing = jnp.sum(
        contract(slot[0], jnp.where(lane == 0, through, 0.0), 1, 0, EXACT)
        + contract(slot[1], jnp.where(lane == 1, through, 0.0), 1, 0, EXACT),
        axis=1,
        keepdims=True,
    )
    feature = [seg[k * rays : (k + 1) * rays] for k in range(K)]
    pass_k = [passing[k * rays : (k + 1) * rays] for k in range(K)]
    rank = [ranks[:, k : k + 1] for k in range(K)]
    ones = jnp.ones((rays, 1), F32)

    def seen(k, skip=None):
        product = ones
        for other in range(K):
            if other != k and other != skip:
                product = product * jnp.where(rank[other] < rank[k], pass_k[other], 1.0)
        return product

    transmit = [seen(k) for k in range(K)]
    ray = jnp.zeros_like(feature[0])
    for k in range(K):
        ray = ray + transmit[k] * feature[k]
    ray_out[...] = ray
    grad = ray - targets[...]
    pull = [jnp.sum(grad * feature[k], axis=1, keepdims=True) for k in range(K)]
    for k in range(K):
        grads[k * rays : (k + 1) * rays, 0:LANES] = transmit[k] * grad
        pass_grad = jnp.zeros((rays, 1), F32)
        for behind in range(K):
            if behind != k:
                pass_grad = pass_grad + jnp.where(
                    rank[k] < rank[behind], pull[behind] * seen(behind, k), 0.0
                )
        grads[k * rays : (k + 1) * rays, LANES : 2 * LANES] = jnp.broadcast_to(
            pass_grad, (rays, LANES)
        )
    spread = None
    for c in range(2):
        both = contract(route[c * bricks : (c + 1) * bricks, :], grads[...], 1, 0, EXACT)
        back[:, c * LANES : (c + 1) * LANES] = both[:, 0:LANES]
        own = jnp.where(lane == c, both[:, LANES : 2 * LANES], 0.0)
        spread = own if spread is None else spread + own
    back[:, 2 * LANES : 3 * LANES] = spread


def rays_step(home, route, ranks, targets):
    return pl.pallas_call(
        rays_kernel,
        out_shape=(
            jax.ShapeDtypeStruct(targets.shape, F32),
            jax.ShapeDtypeStruct(home.shape, F32),
        ),
        scratch_shapes=[pltpu.VMEM((route.shape[1], 2 * LANES), F32)],
        name="rays",
    )(home, route, ranks, targets)


def backward_kernel(
    cot, feats, v1_ref, v2_ref, colors_ref, dens_ref, slope_ref, rows_ref, pose_ref,
    first_w, hidden_w, feature_w, density_w,
    first_g, hidden_g, feature_g, density_g, feat_cot, pose_g,
    color_cot,
):
    sources = cot.shape[0]
    slots = 2 * sources
    seg_cot = jnp.concatenate([cot[:, 0:LANES].T, cot[:, LANES : 2 * LANES].T], axis=1)
    turned = cot[:, 2 * LANES : 3 * LANES].T
    pass_cot = jnp.concatenate([turned[0:1], turned[1:2]], axis=1)
    raw = dens_ref[...]
    depth = (jnp.maximum(raw, 0.0) + jnp.log1p(jnp.exp(-jnp.abs(raw)))) * STEP
    front = jnp.zeros((1, slots), F32)
    weights, kept, pulls = [], [], []
    for s in range(S):
        span = slice(s * slots, (s + 1) * slots)
        e = depth[:, span]
        reach = jnp.exp(-front)
        weight = reach * (1.0 - jnp.exp(-e))
        colors = colors_ref[:, span]
        pulls.append(jnp.sum(colors * seg_cot, axis=0, keepdims=True))
        color_cot[:, span] = (weight * seg_cot * (1.0 - colors * colors)).astype(BF16)
        weights.append(weight)
        kept.append(reach * jnp.exp(-e))
        front = front + e
    behind = pass_cot * jnp.exp(-front)
    depth_cot = [None] * S
    for s in reversed(range(S)):
        depth_cot[s] = pulls[s] * kept[s] - behind
        behind = behind + pulls[s] * weights[s]
    raw_cot = (jnp.concatenate(depth_cot, axis=1) * STEP * jax.nn.sigmoid(raw)).astype(BF16)

    v2 = v2_ref[...]
    gate2 = jax.nn.sigmoid(v2)
    h2 = (v2 * gate2).astype(BF16)
    color_c = color_cot[...]
    feature_g[...] = contract(h2, color_c, 1, 1).astype(BF16).astype(F32)
    density_g[...] = contract(raw_cot, h2, 1, 1).astype(BF16).astype(F32)
    wide = jnp.where(iota((8, 1), 0) == 0, density_w[...].astype(F32), 0.0).astype(BF16)
    wide_cot = jnp.where(iota((8, 1), 0) == 0, raw_cot.astype(F32), 0.0).astype(BF16)
    h2_cot = (
        contract(feature_w[...].astype(BF16), color_c, 1, 0) + contract(wide.T, wide_cot, 1, 0)
    ).astype(BF16).astype(F32)
    v2_cot = (h2_cot * gate2 * (1.0 + v2 * (1.0 - gate2))).astype(BF16)
    v1 = v1_ref[...]
    gate1 = jax.nn.sigmoid(v1)
    h1 = (v1 * gate1).astype(BF16)
    hidden_g[...] = contract(h1, v2_cot, 1, 1).astype(BF16).astype(F32)
    h1_cot = contract(hidden_w[...].astype(BF16), v2_cot, 1, 0).astype(BF16).astype(F32)
    v1_cot = (h1_cot * gate1 * (1.0 + v1 * (1.0 - gate1))).astype(BF16)
    first_g[...] = contract(feats[...], v1_cot, 1, 1).astype(BF16).astype(F32)
    f_cot = contract(first_w[...].astype(BF16), v1_cot, 1, 0).astype(BF16).astype(F32)
    feat_cot[...] = f_cot.T.astype(BF16)

    pull = [
        jnp.sum(slope_ref[a * LANES : (a + 1) * LANES, :] * f_cot, axis=0, keepdims=True)
        for a in range(3)
    ]
    rows = rows_ref[...]
    shift = [jnp.zeros((1, slots), F32)] * 3
    turn = [jnp.zeros((1, slots), F32)] * 3
    for s in range(S):
        distance = rows[6:7] + (s + 0.5) * STEP
        place = [rows[i : i + 1] + distance * rows[3 + i : 4 + i] for i in range(3)]
        part = [pull[a][:, s * slots : (s + 1) * slots] for a in range(3)]
        twist = cross(place, part)
        for a in range(3):
            shift[a] = shift[a] + part[a]
            turn[a] = turn[a] + twist[a]
    sub = iota((8, slots), 0)
    grads = jnp.zeros((8, slots), F32)
    for a in range(3):
        grads = jnp.where(sub == a, turn[a], grads)
        grads = jnp.where(sub == 3 + a, shift[a], grads)
    cams = pose_g.shape[1]
    picked = (iota((cams, slots), 0) == rows[7:8].astype(jnp.int32)).astype(F32)
    pose_g[...] = contract(grads, picked, 1, 1, EXACT)


def backward(cot, saved, slope, rows, pose, weights, cams):
    feats, v1, v2, colors, dens = saved
    count = feats.shape[1]
    outs = [(w.shape, F32) for w in weights]
    outs += [((count, feats.shape[0]), BF16), ((8, cams), F32)]
    return pl.pallas_call(
        backward_kernel,
        out_shape=[jax.ShapeDtypeStruct(shape, kind) for shape, kind in outs],
        scratch_shapes=[pltpu.VMEM((feats.shape[0], count), BF16)],
        compiler_params=pltpu.CompilerParams(vmem_limit_bytes=40 * 2**20),
        name="backward",
    )(cot, feats, v1, v2, colors, dens, slope, rows, pose, *weights)


def plane_kernel(factor, cot, out):
    step = pl.program_id(0)
    count = factor.shape[1]
    row_base, col_base, _, _ = plane_axes(step)
    for part in range(BLOCK // TILE):
        acc = jnp.zeros((TILE, cot.shape[1]), F32)
        for lane in range(0, count, TILE):
            columns = factor[pl.ds(pl.multiple_of(col_base, CELLS), CELLS), lane : lane + TILE]
            tile = table_tile(factor, row_base, part, columns, lane)
            acc = acc + contract(tile, cot[lane : lane + TILE, :], 1, 0)
        out[part * TILE : (part + 1) * TILE, :] = acc


def plane_grads(factor, cot, cells):
    channels = cot.shape[1]
    return pl.pallas_call(
        plane_kernel,
        grid=(cells // BLOCK,),
        in_specs=[whole(factor.shape), whole(cot.shape)],
        out_specs=pl.BlockSpec((BLOCK, channels), lambda step: (step, 0)),
        out_shape=jax.ShapeDtypeStruct((cells, channels), F32),
        compiler_params=pltpu.CompilerParams(vmem_limit_bytes=40 * 2**20),
        name="plane_grads",
    )(factor, cot)


def exchange(rows):
    wide = rows.reshape(rows.shape[0], 1, rows.shape[1])
    moved = lax.all_to_all(wide, AXES, split_axis=0, concat_axis=0, tiled=True)
    return moved.reshape(rows.shape)


def share_sum(part, axis):
    size = lax.axis_size(axis)
    copies = jnp.broadcast_to(part[None], (size,) + part.shape)
    gathered = lax.all_to_all(copies, (axis,), split_axis=0, concat_axis=0, tiled=True)
    return jnp.sum(gathered, axis=0)


def per_device(
    anchors, directions, ray_start, camera_ids, brick_ids, brick_rank, targets,
    planes, first_weight, hidden_weight, feature_weight, density_weight, poses,
):
    bricks = lax.axis_size(AXES)
    table = planes[0]
    weights = (first_weight[0], hidden_weight[0, 0], feature_weight[0], density_weight)
    outgoing, route = dispatch(
        anchors, directions, ray_start[None], camera_ids[None], brick_ids, brick_rank, bricks
    )
    received = exchange(outgoing)
    sent, rows, pose, factor, slope, *saved = forward(received, poses, table, *weights)
    home = exchange(sent)
    feature_slopes = slopes(factor, slope, table)
    ray_feature, back = rays_step(home, route, brick_rank, targets)
    cot = exchange(back)
    first_g, hidden_g, feature_g, density_g, feat_cot, pose_part = backward(
        cot, saved, feature_slopes, rows, pose, weights, poses.shape[1]
    )
    pose_grad = share_sum(share_sum(pose_part, "gy"), "gx")[0:6]
    plane_grad = plane_grads(factor, feat_cot, table.shape[0])
    return (
        ray_feature,
        plane_grad[None],
        first_g[None],
        hidden_g[None, None],
        feature_g[None],
        density_g,
        pose_grad,
    )


def solution(mesh):
    rays = P(AXES)
    in_specs = (
        P(None, AXES), P(None, AXES), rays, rays, P(AXES, None), P(AXES, None), P(AXES, None),
        P(AXES, None, None), P(AXES, None, None), P(AXES, None, None, None), P(AXES, None, None),
        P(AXES, None), P(),
    )
    out_specs = (
        P(AXES, None), P(AXES, None, None), P(AXES, None, None), P(AXES, None, None, None),
        P(AXES, None, None), P(AXES, None), P(),
    )
    return jax.shard_map(
        per_device, mesh=mesh, in_specs=in_specs, out_specs=out_specs, check_vma=False
    )
```

```python
import jax
import jax.numpy as jnp
from jax import lax
from jax.experimental import pallas as pl
from jax.experimental.pallas import tpu as pltpu
from jax.sharding import PartitionSpec as P

K = 4
S = 4
CELLS = 64
LANES = 128
STEP = 0.125
AXES = ("gx", "gy")
F32 = jnp.float32
BF16 = jnp.bfloat16
EXACT = lax.Precision.HIGHEST


def contract(left, right, left_dim, right_dim, precision=None):
    return lax.dot_general(
        left,
        right,
        (((left_dim,), (right_dim,)), ((), ())),
        precision=precision,
        preferred_element_type=F32,
    )


def iota(shape, dim):
    return lax.broadcasted_iota(jnp.int32, shape, dim)


def grant(mebibytes):
    return pltpu.CompilerParams(vmem_limit_bytes=mebibytes * 2**20)


def far(x):
    return pltpu.with_memory_space_constraint(x, pltpu.HBM)


def price(flops, moved):
    return pl.CostEstimate(flops=flops, bytes_accessed=moved, transcendentals=0)


def eye(size):
    return (iota((size, size), 0) == iota((size, size), 1)).astype(F32)


def spread_of(rays):
    segs = rays * K
    spread = (iota((rays, segs), 0) == iota((rays, segs), 1) % rays).astype(F32)
    own = iota((K, segs), 0) == iota((K, segs), 1) // rays
    return spread, own


def segment_row(table, spread, own):
    return jnp.sum(
        jnp.where(own, contract(table[...].astype(F32), spread, 1, 0, EXACT), 0.0), axis=0, keepdims=True
    )


def route_of(id_row, bricks):
    segs = id_row.shape[1]
    onehot = (iota((bricks, segs), 0) == id_row.astype(jnp.int32)).astype(F32)
    earlier = (iota((segs, segs), 0) < iota((segs, segs), 1)).astype(F32)
    before = contract(onehot, earlier, 1, 0)
    return [jnp.where((before > 0.5) == (slot == 1), onehot, 0.0) for slot in range(2)]


def dispatch_kernel(anchors, directions, start, cameras, ids, ranks, out, packed):
    bricks = out.shape[0] // 2
    spread, own = spread_of(anchors.shape[1])
    id_row = segment_row(ids, spread, own)
    packed[0:3, :] = contract(anchors[...], spread, 1, 0, EXACT)
    packed[3:6, :] = contract(directions[...], spread, 1, 0, EXACT)
    packed[6:7, :] = contract(start[...], spread, 1, 0, EXACT) + segment_row(ranks, spread, own) * (S * STEP)
    packed[7:8, :] = contract(cameras[...].astype(F32), spread, 1, 0, EXACT)
    for slot, taken in enumerate(route_of(id_row, bricks)):
        rows = contract(taken, packed[...], 1, 1, EXACT)
        both = jnp.concatenate([rows, jnp.zeros((bricks, LANES - 8), F32)], axis=1)
        out[pl.ds(slot, bricks, stride=2), :] = both


def dispatch(anchors, directions, start, cameras, ids, ranks, bricks):
    return pl.pallas_call(
        dispatch_kernel,
        out_shape=jax.ShapeDtypeStruct((2 * bricks, LANES), F32),
        scratch_shapes=[pltpu.VMEM((8, anchors.shape[1] * K), F32)],
        compiler_params=grant(2),
        name="dispatch",
    )(*map(far, (anchors, directions, start, cameras, ids, ranks)))


def ray_rows(received, poses, sources):
    same = eye(sources)
    rows = jnp.concatenate(
        [
            contract(received[pl.ds(slot, sources, stride=2), :], same, 0, 0, EXACT)[0:8]
            for slot in range(2)
        ],
        axis=1,
    )
    slots = 2 * sources
    cams = poses.shape[1]
    picked = (iota((cams, slots), 0) == rows[7:8].astype(jnp.int32)).astype(F32)
    pose = contract(poses[...], picked, 1, 0, EXACT)
    return rows, picked, pose


def cross(a, b):
    return (
        a[1] * b[2] - a[2] * b[1],
        a[2] * b[0] - a[0] * b[2],
        a[0] * b[1] - a[1] * b[0],
    )


def sample_rows(rows, pose):
    anchor = [rows[i : i + 1] for i in range(3)]
    direction = [rows[3 + i : 4 + i] for i in range(3)]
    turn = [pose[i : i + 1] for i in range(3)]
    shift = [pose[3 + i : 4 + i] for i in range(3)]
    turned = cross(turn, anchor)
    moved = [anchor[i] + turned[i] + shift[i] for i in range(3)]
    bent = cross(turn, direction)
    heading = [direction[i] + bent[i] for i in range(3)]
    distance = [rows[6:7] + (s + 0.5) * STEP for s in range(S)]
    return [
        jnp.concatenate([moved[i] + distance[s] * heading[i] for s in range(S)], axis=1)
        for i in range(3)
    ]


def factors(coordinate):
    count = coordinate.shape[1]
    scaled = coordinate * CELLS
    floor_c = jnp.floor(scaled)
    fraction = scaled - floor_c
    weight = fraction * fraction * (3.0 - 2.0 * fraction)
    slope = (6.0 * CELLS) * fraction * (1.0 - fraction)
    low = lax.bitwise_and(floor_c.astype(jnp.int32), CELLS - 1)
    high = lax.bitwise_and(low + 1, CELLS - 1)
    cell = iota((CELLS, count), 0)
    at_low = cell == low
    at_high = cell == high
    value = jnp.where(at_low, 1.0 - weight, 0.0) + jnp.where(at_high, weight, 0.0)
    change = jnp.where(at_high, slope, 0.0) - jnp.where(at_low, slope, 0.0)
    return value, change


BLOCK = 1024
TILE = 256


def plane_axes(step):
    plane = step // (CELLS * CELLS // BLOCK)
    first = plane // 2
    second = jnp.minimum(plane + 1, 2)
    start = (step % (CELLS * CELLS // BLOCK)) * (BLOCK // CELLS)
    return first * CELLS + start, second * CELLS, first, second


def table_tile(rows_ref, row_base, part, columns, lane):
    pieces = []
    for i in range(TILE // CELLS):
        row = rows_ref[pl.ds(row_base + part * (TILE // CELLS) + i, 1), lane : lane + TILE]
        pieces.append((row * columns).astype(BF16))
    return jnp.concatenate(pieces, axis=0)


def prepare_kernel(
    planes, first_w, hidden_w, feature_w, ids,
    turned, first_o, first_t, hidden_o, hidden_t, feature_o, feature_t, route,
):
    turned[...] = planes[...].T.astype(BF16)

    @pl.when(pl.program_id(0) == 0)
    def _():
        for source, plain, flipped in (
            (first_w, first_o, first_t),
            (hidden_w, hidden_o, hidden_t),
            (feature_w, feature_o, feature_t),
        ):
            plain[...] = source[...].astype(BF16)
            flipped[...] = source[...].T.astype(BF16)
        bricks = route.shape[0] // 2
        spread, own = spread_of(ids.shape[1])
        for slot, taken in enumerate(route_of(segment_row(ids, spread, own), bricks)):
            route[slot * bricks : (slot + 1) * bricks, :] = taken


def whole(shape):
    return pl.BlockSpec(shape, lambda step: (0,) * len(shape))


def prepare(planes, first_w, hidden_w, feature_w, ids, bricks):
    cells, channels = planes.shape
    ins = [planes, first_w, hidden_w, feature_w, ids]
    outs = [((channels, cells), BF16)]
    for w in (first_w, hidden_w, feature_w):
        outs += [(w.shape, BF16), (w.shape[::-1], BF16)]
    outs += [((2 * bricks, ids.shape[1] * K), F32)]
    in_specs = [whole(x.shape) for x in ins]
    in_specs[0] = pl.BlockSpec((2 * BLOCK, channels), lambda step: (step, 0))
    out_specs = [whole(shape) for shape, _ in outs]
    out_specs[0] = pl.BlockSpec((channels, 2 * BLOCK), lambda step: (0, step))
    return pl.pallas_call(
        prepare_kernel,
        grid=(cells // (2 * BLOCK),),
        in_specs=in_specs,
        out_specs=out_specs,
        out_shape=[pltpu.HBM(shape, kind) for shape, kind in outs],
        compiler_params=grant(8),
        cost_estimate=price(0, 10 * 2**20),
        name="prepare",
    )(*map(far, ins))


def fetch(sources, places, sems, first=0):
    copies = [
        pltpu.make_async_copy(source, place, sems.at[first + i])
        for i, (source, place) in enumerate(zip(sources, places))
    ]
    for copy in copies:
        copy.start()
    return copies


def turned_copies(turned, held, sems, first_step, last_step):
    def copy(step):
        start = pl.multiple_of(step * BLOCK, BLOCK)
        local = pl.multiple_of((step - first_step) * BLOCK, BLOCK)
        return pltpu.make_async_copy(
            turned.at[:, pl.ds(start, BLOCK)], held.at[:, pl.ds(local, BLOCK)], sems.at[step - first_step]
        )

    for step in range(first_step, last_step):
        copy(step).start()
    return copy


def plane_tile(held, step, part):
    return held[:, pl.ds(pl.multiple_of(step * BLOCK + part * TILE, TILE), TILE)]


def forward_kernel(
    received, poses_h, turned_h, first_h, hidden_h, feature_h, density_h,
    out, rows_h, points_h, feats_h, v1_h, v2_h, colors_h, dens_h,
    poses, turned, first_t, hidden_t, feature_t, density_w,
    rows_v, points_v, feats_v, v1_v, v2_v, colors_v, dens_v,
    factor, total, plane_sems, in_sems, out_sems,
):
    sources = received.shape[0] // 2
    slots = 2 * sources
    count = slots * S
    steps = turned.shape[1] // BLOCK
    arriving = fetch(
        (poses_h, first_h, hidden_h, feature_h, density_h),
        (poses, first_t, hidden_t, feature_t, density_w),
        in_sems,
    )
    plane_copy = turned_copies(turned_h, turned, plane_sems, 0, steps)
    arriving[0].wait()
    rows, _, pose = ray_rows(received, poses, sources)
    rows_v[...] = rows
    points = sample_rows(rows, pose)
    for axis, coordinate in enumerate(points):
        factor[axis * CELLS : (axis + 1) * CELLS, :] = factors(coordinate)[0]
        points_v[axis : axis + 1, :] = coordinate
    points_v[3:8, :] = jnp.zeros((5, count), F32)
    leaving = fetch((rows_v, points_v), (rows_h, points_h), out_sems)
    total[...] = jnp.zeros_like(total)

    @pl.loop(0, steps)
    def _(step):
        plane_copy(step).wait()
        row_base, col_base, _, _ = plane_axes(step)
        for lane in range(0, count, TILE):
            columns = factor[pl.ds(pl.multiple_of(col_base, CELLS), CELLS), lane : lane + TILE]
            acc = total[:, lane : lane + TILE]
            for part in range(BLOCK // TILE):
                tile = table_tile(factor, row_base, part, columns, lane)
                acc = acc + contract(plane_tile(turned, step, part), tile, 1, 0)
            total[:, lane : lane + TILE] = acc

    for copy in arriving[1:]:
        copy.wait()
    feats = total[...].astype(BF16)
    feats_v[...] = feats
    v1 = contract(first_t[...], feats, 1, 0)
    v1_v[...] = v1
    leaving += fetch((feats_v, v1_v), (feats_h, v1_h), out_sems, 2)
    h1 = (v1 * jax.nn.sigmoid(v1)).astype(BF16)
    v2 = contract(hidden_t[...], h1, 1, 0)
    v2_v[...] = v2
    leaving += fetch((v2_v,), (v2_h,), out_sems, 4)
    h2 = (v2 * jax.nn.sigmoid(v2)).astype(BF16)
    colors = jnp.tanh(contract(feature_t[...], h2, 1, 0))
    colors_v[...] = colors
    raw = contract(density_w[...].astype(BF16), h2, 1, 0)
    dens_v[...] = raw
    leaving += fetch((colors_v, dens_v), (colors_h, dens_h), out_sems, 5)
    depth = (jnp.maximum(raw, 0.0) + jnp.log1p(jnp.exp(-jnp.abs(raw)))) * STEP
    seg = jnp.zeros((LANES, slots), F32)
    front = jnp.zeros((1, slots), F32)
    for s in range(S):
        e = depth[:, s * slots : (s + 1) * slots]
        weight = jnp.exp(-front) * (1.0 - jnp.exp(-e))
        seg = seg + weight * colors[:, s * slots : (s + 1) * slots]
        front = front + e
    through = jnp.exp(-front)
    out[pl.ds(0, sources, stride=3), :] = seg[:, 0:sources].T
    out[pl.ds(1, sources, stride=3), :] = seg[:, sources:slots].T
    sub = iota((8, sources), 0)
    both = jnp.where(
        sub == 0, through[:, 0:sources], jnp.where(sub == 1, through[:, sources:slots], 0.0)
    )
    place = (iota((8, LANES), 0) == iota((8, LANES), 1)).astype(F32)
    out[pl.ds(2, sources, stride=3), :] = contract(both, place, 0, 0, EXACT)
    for copy in leaving:
        copy.wait()


IN_HBM = pl.BlockSpec(memory_space=pltpu.HBM)
IN_VMEM = pl.BlockSpec(memory_space=pltpu.VMEM)


def forward(received, poses, turned, first_t, hidden_t, feature_t, density_w):
    sources = received.shape[0] // 2
    slots = 2 * sources
    count = slots * S
    channels, cells = turned.shape
    hidden = first_t.shape[0]
    saved = [
        ((8, slots), F32),
        ((8, count), F32),
        ((channels, count), BF16),
        ((hidden, count), F32),
        ((hidden, count), F32),
        ((channels, count), F32),
        ((1, count), F32),
    ]
    params = [poses, turned, first_t, hidden_t, feature_t, density_w]
    return pl.pallas_call(
        forward_kernel,
        in_specs=[IN_VMEM] + [IN_HBM] * len(params),
        out_specs=[IN_VMEM] + [IN_HBM] * len(saved),
        out_shape=[jax.ShapeDtypeStruct((3 * sources, LANES), F32)]
        + [pltpu.HBM(shape, kind) for shape, kind in saved],
        scratch_shapes=[pltpu.VMEM(x.shape, x.dtype) for x in params]
        + [pltpu.VMEM(shape, kind) for shape, kind in saved]
        + [
            pltpu.VMEM((3 * CELLS, count), F32),
            pltpu.VMEM((channels, count), F32),
            pltpu.SemaphoreType.DMA((cells // BLOCK,)),
            pltpu.SemaphoreType.DMA((5,)),
            pltpu.SemaphoreType.DMA((7,)),
        ],
        compiler_params=grant(24),
        cost_estimate=price(2 * cells * count * channels, 8 * 2**20),
        name="forward",
    )(received, *map(far, params))


def slopes(points, turned, first_step, last_step):
    count = points.shape[1]
    channels = turned.shape[0]
    steps = last_step - first_step

    def slope_kernel(points, turned_h, out, held, factor, slope, total, sems):
        plane_copy = turned_copies(turned_h, held, sems, first_step, last_step)
        for axis in range(3):
            span = slice(axis * CELLS, (axis + 1) * CELLS)
            factor[span, :], slope[span, :] = factors(points[axis : axis + 1, :])
        total[...] = jnp.zeros_like(total)

        @pl.loop(first_step, last_step)
        def _(step):
            plane_copy(step).wait()
            row_base, col_base, first, second = plane_axes(step)
            for rows_ref, cols_ref, axis in ((slope, factor, first), (factor, slope, second)):
                base = pl.multiple_of(axis * LANES, LANES)
                for lane in range(0, count, TILE):
                    columns = cols_ref[
                        pl.ds(pl.multiple_of(col_base, CELLS), CELLS), lane : lane + TILE
                    ]
                    acc = total[pl.ds(base, LANES), lane : lane + TILE]
                    for part in range(BLOCK // TILE):
                        tile = table_tile(rows_ref, row_base, part, columns, lane)
                        acc = acc + contract(plane_tile(held, step - first_step, part), tile, 1, 0)
                    total[pl.ds(base, LANES), lane : lane + TILE] = acc

        out[...] = total[...].astype(BF16)

    return pl.pallas_call(
        slope_kernel,
        in_specs=[IN_VMEM, IN_HBM],
        out_shape=pltpu.HBM((3 * channels, count), BF16),
        scratch_shapes=[
            pltpu.VMEM((channels, steps * BLOCK), BF16),
            pltpu.VMEM((3 * CELLS, count), F32),
            pltpu.VMEM((3 * CELLS, count), F32),
            pltpu.VMEM((3 * channels, count), F32),
            pltpu.SemaphoreType.DMA((steps,)),
        ],
        compiler_params=grant(16),
        cost_estimate=price(4 * steps * BLOCK * count * channels, 6 * 2**20),
        name="slopes",
    )(far(points), far(turned))


def rays_kernel(home, route, ranks, targets, ray_out, back, grads):
    bricks = home.shape[0] // 3
    rays = targets.shape[0]
    slot = [route[0:bricks, :].T, route[bricks : 2 * bricks, :].T]
    seg = contract(slot[0], home[pl.ds(0, bricks, stride=3), :], 1, 0, EXACT) + contract(
        slot[1], home[pl.ds(1, bricks, stride=3), :], 1, 0, EXACT
    )
    lane = iota((1, LANES), 1)
    through = home[pl.ds(2, bricks, stride=3), :]
    passing = jnp.sum(
        contract(slot[0], jnp.where(lane == 0, through, 0.0), 1, 0, EXACT)
        + contract(slot[1], jnp.where(lane == 1, through, 0.0), 1, 0, EXACT),
        axis=1,
        keepdims=True,
    )
    feature = [seg[k * rays : (k + 1) * rays] for k in range(K)]
    pass_k = [passing[k * rays : (k + 1) * rays] for k in range(K)]
    rank_cols = contract(eye(rays), ranks[...].astype(F32), 1, 1, EXACT)
    rank = [rank_cols[:, k : k + 1] for k in range(K)]
    ones = jnp.ones((rays, 1), F32)

    def seen(k, skip=None):
        product = ones
        for other in range(K):
            if other != k and other != skip:
                product = product * jnp.where(rank[other] < rank[k], pass_k[other], 1.0)
        return product

    transmit = [seen(k) for k in range(K)]
    ray = jnp.zeros_like(feature[0])
    for k in range(K):
        ray = ray + transmit[k] * feature[k]
    ray_out[...] = ray
    grad = ray - targets[...]
    pull = [jnp.sum(grad * feature[k], axis=1, keepdims=True) for k in range(K)]
    for k in range(K):
        grads[k * rays : (k + 1) * rays, 0:LANES] = transmit[k] * grad
        pass_grad = jnp.zeros((rays, 1), F32)
        for behind in range(K):
            if behind != k:
                pass_grad = pass_grad + jnp.where(
                    rank[k] < rank[behind], pull[behind] * seen(behind, k), 0.0
                )
        grads[k * rays : (k + 1) * rays, LANES : 2 * LANES] = jnp.broadcast_to(
            pass_grad, (rays, LANES)
        )
    spread = None
    for c in range(2):
        both = contract(route[c * bricks : (c + 1) * bricks, :], grads[...], 1, 0, EXACT)
        back[pl.ds(c, bricks, stride=3), :] = both[:, 0:LANES]
        own = jnp.where(lane == c, both[:, LANES : 2 * LANES], 0.0)
        spread = own if spread is None else spread + own
    back[pl.ds(2, bricks, stride=3), :] = spread


def rays_step(home, route, ranks, targets):
    return pl.pallas_call(
        rays_kernel,
        out_shape=(
            pltpu.HBM(targets.shape, F32),
            jax.ShapeDtypeStruct(home.shape, F32),
        ),
        scratch_shapes=[pltpu.VMEM((route.shape[1], 2 * LANES), F32)],
        compiler_params=grant(4),
        name="rays",
    )(home, *map(far, (route, ranks, targets)))


def backward_kernel(
    cot, dens_h, colors_h, v2_h, feature_h, density_h, v1_h, hidden_h, feats_h, first_h, rows_h, slope_ah, slope_bh,
    pose_g, feature_gh, density_gh, hidden_gh, first_gh, feat_cot_h,
    dens_ref, colors_ref, v2_ref, feature_w, density_w, v1_ref, hidden_w, feats, first_w, rows_ref, slope_a, slope_b,
    feature_g, density_g, hidden_g, first_g, feat_cot,
    color_cot, in_sems, out_sems,
):
    arriving = fetch(
        (dens_h, colors_h, v2_h, feature_h, density_h, v1_h, hidden_h, feats_h, first_h, rows_h, slope_ah, slope_bh),
        (dens_ref, colors_ref, v2_ref, feature_w, density_w, v1_ref, hidden_w, feats, first_w, rows_ref, slope_a, slope_b),
        in_sems,
    )
    sources = cot.shape[0] // 3
    slots = 2 * sources
    seg_cot = jnp.concatenate(
        [cot[pl.ds(slot, sources, stride=3), :].T for slot in range(2)], axis=1
    )
    turned = cot[pl.ds(2, sources, stride=3), :].T
    pass_cot = jnp.concatenate([turned[0:1], turned[1:2]], axis=1)
    arriving[0].wait()
    arriving[1].wait()
    raw = dens_ref[...]
    depth = (jnp.maximum(raw, 0.0) + jnp.log1p(jnp.exp(-jnp.abs(raw)))) * STEP
    front = jnp.zeros((1, slots), F32)
    weights, kept, pulls = [], [], []
    for s in range(S):
        span = slice(s * slots, (s + 1) * slots)
        e = depth[:, span]
        reach = jnp.exp(-front)
        weight = reach * (1.0 - jnp.exp(-e))
        colors = colors_ref[:, span]
        pulls.append(jnp.sum(colors * seg_cot, axis=0, keepdims=True))
        color_cot[:, span] = (weight * seg_cot * (1.0 - colors * colors)).astype(BF16)
        weights.append(weight)
        kept.append(reach * jnp.exp(-e))
        front = front + e
    behind = pass_cot * jnp.exp(-front)
    depth_cot = [None] * S
    for s in reversed(range(S)):
        depth_cot[s] = pulls[s] * kept[s] - behind
        behind = behind + pulls[s] * weights[s]
    raw_cot = (jnp.concatenate(depth_cot, axis=1) * STEP * jax.nn.sigmoid(raw)).astype(BF16)

    for copy in arriving[2:5]:
        copy.wait()
    v2 = v2_ref[...]
    gate2 = jax.nn.sigmoid(v2)
    h2 = (v2 * gate2).astype(BF16)
    color_c = color_cot[...]
    feature_g[...] = contract(h2, color_c, 1, 1).astype(BF16).astype(F32)
    density_g[...] = contract(raw_cot, h2, 1, 1).astype(BF16).astype(F32)
    leaving = fetch((feature_g, density_g), (feature_gh, density_gh), out_sems)
    wide = jnp.where(iota((8, 1), 0) == 0, density_w[...].astype(F32), 0.0).astype(BF16)
    wide_cot = jnp.where(iota((8, 1), 0) == 0, raw_cot.astype(F32), 0.0).astype(BF16)
    h2_cot = (
        contract(feature_w[...], color_c, 1, 0) + contract(wide.T, wide_cot, 1, 0)
    ).astype(BF16).astype(F32)
    v2_cot = (h2_cot * gate2 * (1.0 + v2 * (1.0 - gate2))).astype(BF16)
    for copy in arriving[5:9]:
        copy.wait()
    v1 = v1_ref[...]
    gate1 = jax.nn.sigmoid(v1)
    h1 = (v1 * gate1).astype(BF16)
    hidden_g[...] = contract(h1, v2_cot, 1, 1).astype(BF16).astype(F32)
    leaving += fetch((hidden_g,), (hidden_gh,), out_sems, 2)
    h1_cot = contract(hidden_w[...], v2_cot, 1, 0).astype(BF16).astype(F32)
    v1_cot = (h1_cot * gate1 * (1.0 + v1 * (1.0 - gate1))).astype(BF16)
    first_g[...] = contract(feats[...], v1_cot, 1, 1).astype(BF16).astype(F32)
    f_cot = contract(first_w[...], v1_cot, 1, 0).astype(BF16).astype(F32)
    feat_cot[...] = f_cot.T.astype(BF16)
    leaving += fetch((first_g, feat_cot), (first_gh, feat_cot_h), out_sems, 3)
    for copy in arriving[9:]:
        copy.wait()

    pull = [
        jnp.sum(
            (
                slope_a[a * LANES : (a + 1) * LANES, :].astype(F32)
                + slope_b[a * LANES : (a + 1) * LANES, :].astype(F32)
            )
            * f_cot,
            axis=0,
            keepdims=True,
        )
        for a in range(3)
    ]
    rows = rows_ref[...]
    shift = [jnp.zeros((1, slots), F32)] * 3
    turn = [jnp.zeros((1, slots), F32)] * 3
    for s in range(S):
        distance = rows[6:7] + (s + 0.5) * STEP
        place = [rows[i : i + 1] + distance * rows[3 + i : 4 + i] for i in range(3)]
        part = [pull[a][:, s * slots : (s + 1) * slots] for a in range(3)]
        twist = cross(place, part)
        for a in range(3):
            shift[a] = shift[a] + part[a]
            turn[a] = turn[a] + twist[a]
    sub = iota((8, slots), 0)
    grads = jnp.zeros((8, slots), F32)
    for a in range(3):
        grads = jnp.where(sub == a, turn[a], grads)
        grads = jnp.where(sub == 3 + a, shift[a], grads)
    cams = pose_g.shape[1]
    picked = (iota((cams, slots), 0) == rows[7:8].astype(jnp.int32)).astype(F32)
    pose = contract(grads, picked, 1, 1, EXACT)
    for copy in range(pose_g.shape[0] // 8):
        pose_g[copy * 8 : (copy + 1) * 8, :] = pose
    for copy in leaving:
        copy.wait()


def backward(cot, saved, slope_a, slope_b, rows, weights, cams, copies):
    feats, v1, v2, colors, dens = saved
    first_w, hidden_w, feature_w, density_w = weights
    channels, count = feats.shape
    ins = [dens, colors, v2, feature_w, density_w, v1, hidden_w, feats, first_w, rows, slope_a, slope_b]
    outs = [(w.shape, F32) for w in (feature_w, density_w, hidden_w, first_w)] + [((count, channels), BF16)]
    return pl.pallas_call(
        backward_kernel,
        in_specs=[IN_VMEM] + [IN_HBM] * len(ins),
        out_specs=[IN_VMEM] + [IN_HBM] * len(outs),
        out_shape=[jax.ShapeDtypeStruct((8 * copies, cams), F32)]
        + [pltpu.HBM(shape, kind) for shape, kind in outs],
        scratch_shapes=[pltpu.VMEM(x.shape, x.dtype) for x in ins]
        + [pltpu.VMEM(shape, kind) for shape, kind in outs]
        + [
            pltpu.VMEM((channels, count), BF16),
            pltpu.SemaphoreType.DMA((len(ins),)),
            pltpu.SemaphoreType.DMA((len(outs),)),
        ],
        compiler_params=grant(24),
        name="backward",
    )(cot, *map(far, ins))


def plane_grads(points, cot, cells, first_step, last_step, begun=None):
    count = points.shape[1]
    channels = cot.shape[1]

    def plane_kernel(points, cot, *rest):
        out, factor = rest[-2:]

        @pl.when(pl.program_id(0) == 0)
        def _():
            for axis in range(3):
                factor[axis * CELLS : (axis + 1) * CELLS, :] = factors(points[axis : axis + 1, :])[0]

        row_base, col_base, _, _ = plane_axes(pl.program_id(0) + first_step)
        for part in range(BLOCK // TILE):
            acc = jnp.zeros((TILE, channels), F32)
            for lane in range(0, count, TILE):
                columns = factor[pl.ds(pl.multiple_of(col_base, CELLS), CELLS), lane : lane + TILE]
                tile = table_tile(factor, row_base, part, columns, lane)
                acc = acc + contract(tile, cot[lane : lane + TILE, :], 1, 0)
            out[part * TILE : (part + 1) * TILE, :] = acc

    steps = last_step - first_step
    earlier = [] if begun is None else [begun]
    return pl.pallas_call(
        plane_kernel,
        grid=(steps,),
        in_specs=[whole(points.shape), whole(cot.shape)] + [IN_HBM] * len(earlier),
        out_specs=pl.BlockSpec((BLOCK, channels), lambda step: (step + first_step, 0)),
        out_shape=pltpu.HBM((cells, channels), F32),
        scratch_shapes=[pltpu.VMEM((3 * CELLS, count), F32)],
        input_output_aliases={2: 0} if earlier else {},
        compiler_params=grant(8),
        cost_estimate=price(2 * steps * BLOCK * count * channels, steps * BLOCK * channels * 4),
        name="plane_grads",
    )(far(points), far(cot), *map(far, earlier))


def exchange(rows, peers):
    wide = rows.reshape(peers, 1, rows.size // peers)
    moved = lax.all_to_all(wide, AXES, split_axis=0, concat_axis=0, tiled=True)
    return moved.reshape(rows.shape)


def swap(copies, axis):
    stacked = copies.reshape(lax.axis_size(axis), 8, copies.shape[1])
    moved = lax.all_to_all(stacked, (axis,), split_axis=0, concat_axis=0, tiled=True)
    return moved.reshape(copies.shape)


def add_kernel(parts, out):
    total = parts[0:8, :]
    for source in range(1, parts.shape[0] // 8):
        total = total + parts[source * 8 : (source + 1) * 8, :]
    rows = min(8, out.shape[0])
    for copy in range(out.shape[0] // rows):
        out[copy * rows : (copy + 1) * rows, :] = total[0:rows]


def add(parts, out_shape):
    return pl.pallas_call(
        add_kernel, out_shape=out_shape, compiler_params=grant(2), name="add"
    )(parts)


def per_device(
    anchors, directions, ray_start, camera_ids, brick_ids, brick_rank, targets,
    planes, first_weight, hidden_weight, feature_weight, density_weight, poses,
):
    bricks = lax.axis_size(AXES)
    cells = planes.shape[1]
    steps = cells // BLOCK
    cams = poses.shape[1]
    ids, ranks = brick_ids.T, brick_rank.T
    outgoing = dispatch(anchors, directions, ray_start[None], camera_ids[None], ids, ranks, bricks)
    received = exchange(outgoing, bricks)
    turned, first_o, first_t, hidden_o, hidden_t, feature_o, feature_t, route = prepare(
        planes[0], first_weight[0], hidden_weight[0, 0], feature_weight[0], ids, bricks
    )
    sent, rows, points, *saved = forward(
        received, poses, turned, first_t, hidden_t, feature_t, density_weight
    )
    home = exchange(sent, bricks)
    slope_a = slopes(points, turned, 0, steps // 2)
    ray_feature, back = rays_step(home, route, ranks, targets)
    cot = exchange(back, bricks)
    later_points, back = lax.optimization_barrier((points, back))
    slope_b = slopes(later_points, turned, steps // 2, steps)
    pose_part, feature_g, density_g, hidden_g, first_g, feat_cot = backward(
        cot, saved, slope_a, slope_b, rows, (first_o, hidden_o, feature_o, density_weight), cams, lax.axis_size("gy")
    )
    column_parts = swap(pose_part, "gy")
    plane_grad = plane_grads(points, feat_cot, cells, 0, steps // 2)
    column_sum = add(column_parts, jax.ShapeDtypeStruct((8 * lax.axis_size("gx"), cams), F32))
    later_cot, column_sum = lax.optimization_barrier((feat_cot, column_sum))
    pose_grad = add(swap(column_sum, "gx"), pltpu.HBM(poses.shape, F32))
    plane_grad = plane_grads(points, later_cot, cells, steps // 2, steps, plane_grad)
    return (
        ray_feature,
        plane_grad[None],
        first_g[None],
        hidden_g[None, None],
        feature_g[None],
        density_g,
        pose_grad,
    )


def solution(mesh):
    rays = P(AXES)
    in_specs = (
        P(None, AXES), P(None, AXES), rays, rays, P(AXES, None), P(AXES, None), P(AXES, None),
        P(AXES, None, None), P(AXES, None, None), P(AXES, None, None, None), P(AXES, None, None),
        P(AXES, None), P(),
    )
    out_specs = (
        P(AXES, None), P(AXES, None, None), P(AXES, None, None), P(AXES, None, None, None),
        P(AXES, None, None), P(AXES, None), P(),
    )
    return jax.shard_map(
        per_device, mesh=mesh, in_specs=in_specs, out_specs=out_specs, check_vma=False
    )
```

```python
import jax
import jax.numpy as jnp
from jax import lax
from jax.experimental import pallas as pl
from jax.experimental.pallas import tpu as pltpu
from jax.sharding import PartitionSpec as P

K = 4
S = 4
CELLS = 64
LANES = 128
STEP = 0.125
AXES = ("gx", "gy")
F32 = jnp.float32
BF16 = jnp.bfloat16
EXACT = lax.Precision.HIGHEST


def contract(left, right, left_dim, right_dim, precision=None):
    return lax.dot_general(
        left,
        right,
        (((left_dim,), (right_dim,)), ((), ())),
        precision=precision,
        preferred_element_type=F32,
    )


def iota(shape, dim):
    return lax.broadcasted_iota(jnp.int32, shape, dim)


def grant(mebibytes):
    return pltpu.CompilerParams(vmem_limit_bytes=mebibytes * 2**20)


def far(x):
    return pltpu.with_memory_space_constraint(x, pltpu.HBM)


def price(flops, moved):
    return pl.CostEstimate(flops=flops, bytes_accessed=moved, transcendentals=0)


def select_rows(onehot, values, left_dim, right_dim, parts=3):
    picked = onehot.astype(BF16)
    total = None
    rest = values
    for _ in range(parts):
        part = rest.astype(BF16)
        rest = rest - part.astype(F32)
        term = contract(picked, part, left_dim, right_dim)
        total = term if total is None else total + term
    return total


def eye(size):
    return (iota((size, size), 0) == iota((size, size), 1)).astype(F32)


def spread_of(rays):
    segs = rays * K
    spread = (iota((rays, segs), 0) == iota((rays, segs), 1) % rays).astype(F32)
    own = iota((K, segs), 0) == iota((K, segs), 1) // rays
    return spread, own


def segment_row(table, spread, own):
    four = contract(table[...].astype(F32).astype(BF16), spread.astype(BF16), 1, 0)
    return jnp.sum(jnp.where(own, four, 0.0), axis=0, keepdims=True)


def route_of(id_row, bricks):
    segs = id_row.shape[1]
    onehot = (iota((bricks, segs), 0) == id_row.astype(jnp.int32)).astype(F32)
    earlier = (iota((segs, segs), 0) < iota((segs, segs), 1)).astype(F32)
    before = contract(onehot.astype(BF16), earlier.astype(BF16), 1, 0)
    return [jnp.where((before > 0.5) == (slot == 1), onehot, 0.0) for slot in range(2)]


def cross(a, b):
    return (
        a[1] * b[2] - a[2] * b[1],
        a[2] * b[0] - a[0] * b[2],
        a[0] * b[1] - a[1] * b[0],
    )


def dispatch_kernel(anchors, directions, start, cameras, ids, ranks, poses, out, packed):
    bricks = out.shape[0] // 2
    rays = anchors.shape[1]
    spread, own = spread_of(rays)
    id_row = segment_row(ids, spread, own)
    picked = (iota((poses.shape[1], rays), 0) == cameras[...]).astype(F32)
    pose = contract(poses[...], picked, 1, 0, EXACT)
    turn = [pose[i : i + 1] for i in range(3)]
    anchor = [anchors[i : i + 1, :] for i in range(3)]
    direction = [directions[i : i + 1, :] for i in range(3)]
    turned = cross(turn, anchor)
    bent = cross(turn, direction)
    for i in range(3):
        packed[i : i + 1, :] = anchor[i] + turned[i] + pose[3 + i : 4 + i]
        packed[3 + i : 4 + i, :] = direction[i] + bent[i]
    packed[6:9, :] = anchors[...]
    packed[9:12, :] = directions[...]
    packed[12:13, :] = start[...]
    packed[13:14, :] = cameras[...].astype(F32)
    packed[14:16, :] = jnp.zeros((2, rays), F32)
    rank_row = segment_row(ranks, spread, own)
    values = contract(packed[...], spread, 1, 0, EXACT)
    values = values + jnp.where(iota((16, 1), 0) == 12, rank_row * (S * STEP), 0.0)
    for slot, taken in enumerate(route_of(id_row, bricks)):
        rows = select_rows(taken, values, 1, 1)
        both = jnp.concatenate([rows, jnp.zeros((bricks, LANES - 16), F32)], axis=1)
        out[pl.ds(slot, bricks, stride=2), :] = both


def dispatch(anchors, directions, start, cameras, ids, ranks, poses, bricks):
    return pl.pallas_call(
        dispatch_kernel,
        out_shape=jax.ShapeDtypeStruct((2 * bricks, LANES), F32),
        scratch_shapes=[pltpu.VMEM((16, anchors.shape[1]), F32)],
        compiler_params=grant(2),
        name="dispatch",
    )(*map(far, (anchors, directions, start, cameras, ids, ranks, poses)))


def ray_rows(received, sources):
    same = eye(sources)
    return jnp.concatenate(
        [
            contract(received[pl.ds(slot, sources, stride=2), :], same, 0, 0, EXACT)[0:16]
            for slot in range(2)
        ],
        axis=1,
    )


def sample_rows(rows):
    distance = [rows[12:13] + (s + 0.5) * STEP for s in range(S)]
    return [
        jnp.concatenate(
            [rows[i : i + 1] + distance[s] * rows[3 + i : 4 + i] for s in range(S)], axis=1
        )
        for i in range(3)
    ]


def factors(coordinate):
    count = coordinate.shape[1]
    scaled = coordinate * CELLS
    floor_c = jnp.floor(scaled)
    fraction = scaled - floor_c
    weight = fraction * fraction * (3.0 - 2.0 * fraction)
    slope = (6.0 * CELLS) * fraction * (1.0 - fraction)
    low = lax.bitwise_and(floor_c.astype(jnp.int32), CELLS - 1)
    high = lax.bitwise_and(low + 1, CELLS - 1)
    cell = iota((CELLS, count), 0)
    at_low = cell == low
    at_high = cell == high
    value = jnp.where(at_low, 1.0 - weight, 0.0) + jnp.where(at_high, weight, 0.0)
    change = jnp.where(at_high, slope, 0.0) - jnp.where(at_low, slope, 0.0)
    return value, change


BLOCK = 1024
TILE = 256


def plane_axes(step):
    plane = step // (CELLS * CELLS // BLOCK)
    first = plane // 2
    second = jnp.minimum(plane + 1, 2)
    start = (step % (CELLS * CELLS // BLOCK)) * (BLOCK // CELLS)
    return first * CELLS + start, second * CELLS, first, second


def table_tile(rows_ref, row_base, part, columns, lane):
    pieces = []
    for i in range(TILE // CELLS):
        row = rows_ref[pl.ds(row_base + part * (TILE // CELLS) + i, 1), lane : lane + TILE]
        pieces.append((row * columns).astype(BF16))
    return jnp.concatenate(pieces, axis=0)


IN_HBM = pl.BlockSpec(memory_space=pltpu.HBM)
IN_VMEM = pl.BlockSpec(memory_space=pltpu.VMEM)


def shapes(*arrays):
    return [jax.ShapeDtypeStruct(x.shape, x.dtype) for x in arrays]


def fetch(sources, places, sems, first=0):
    copies = [
        pltpu.make_async_copy(source, place, sems.at[first + i])
        for i, (source, place) in enumerate(zip(sources, places))
    ]
    for copy in copies:
        copy.start()
    return copies


def plane_copies(planes, held, sems, first_step, last_step):
    def copy(step):
        start = pl.multiple_of(step * BLOCK, BLOCK)
        local = pl.multiple_of((step - first_step) * BLOCK, BLOCK)
        return pltpu.make_async_copy(
            planes.at[pl.ds(start, BLOCK), :], held.at[pl.ds(local, BLOCK), :], sems.at[step - first_step]
        )

    for step in range(first_step, last_step):
        copy(step).start()
    return copy


def prepare_kernel(
    planes, first_h, hidden_h, feature_h, density_h, ids_h,
    turned, first_t, hidden_t, feature_t, density_w, first_oh, hidden_oh, feature_oh, route_h,
    held, first_w, hidden_w, feature_w, ids, first_o, hidden_o, feature_o, route, plane_sems, in_sems, out_sems,
):
    steps = planes.shape[0] // BLOCK
    arriving = fetch(
        (ids_h, first_h, hidden_h, feature_h, density_h), (ids, first_w, hidden_w, feature_w, density_w), in_sems
    )
    plane_copy = plane_copies(planes, held, plane_sems, 0, steps)
    for copy in arriving:
        copy.wait()
    for source, plain, flipped in (
        (first_w, first_o, first_t),
        (hidden_w, hidden_o, hidden_t),
        (feature_w, feature_o, feature_t),
    ):
        plain[...] = source[...].astype(BF16)
        flipped[...] = source[...].T.astype(BF16)
    bricks = route.shape[0] // 4
    spread, own = spread_of(ids.shape[1])
    for slot, taken in enumerate(route_of(segment_row(ids, spread, own), bricks)):
        route[slot * bricks : (slot + 1) * bricks, :] = taken.astype(BF16)
        route[(2 + slot) * bricks : (3 + slot) * bricks, :] = taken.T.astype(BF16)
    leaving = fetch((first_o, hidden_o, feature_o, route), (first_oh, hidden_oh, feature_oh, route_h), out_sems)

    @pl.loop(0, steps)
    def _(step):
        plane_copy(step).wait()
        span = pl.ds(pl.multiple_of(step * BLOCK, BLOCK), BLOCK)
        turned[:, span] = held[span, :].T.astype(BF16)

    for copy in leaving:
        copy.wait()


def prepare(planes, first_w, hidden_w, feature_w, density_w, ids, bricks):
    cells, channels = planes.shape
    flips = [jax.ShapeDtypeStruct(w.shape[::-1], BF16) for w in (first_w, hidden_w, feature_w)]
    plains = [pltpu.HBM(w.shape, BF16) for w in (first_w, hidden_w, feature_w)]
    return pl.pallas_call(
        prepare_kernel,
        in_specs=[IN_HBM] * 6,
        out_specs=[IN_VMEM] * 5 + [IN_HBM] * 4,
        out_shape=[jax.ShapeDtypeStruct((channels, cells), BF16)]
        + flips
        + shapes(density_w)
        + plains
        + [pltpu.HBM((4 * bricks, ids.shape[1] * K), BF16)],
        scratch_shapes=[pltpu.VMEM((cells, channels), F32)]
        + [pltpu.VMEM(x.shape, x.dtype) for x in (first_w, hidden_w, feature_w, ids)]
        + [pltpu.VMEM(w.shape, BF16) for w in (first_w, hidden_w, feature_w)]
        + [
            pltpu.VMEM((4 * bricks, ids.shape[1] * K), BF16),
            pltpu.SemaphoreType.DMA((cells // BLOCK,)),
            pltpu.SemaphoreType.DMA((5,)),
            pltpu.SemaphoreType.DMA((4,)),
        ],
        compiler_params=grant(16),
        cost_estimate=price(0, 10 * 2**20),
        name="prepare",
    )(*map(far, (planes, first_w, hidden_w, feature_w, density_w, ids)))


def forward_kernel(
    received, turned, first_t, hidden_t, feature_t, density_w,
    out_h, rows_h, points_h, feats_h, v1_h, v2_h, colors_h,
    out, rows_v, points_v, feats_v, v1_v, v2_v, colors_v,
    factor, total, out_sems,
):
    sources = received.shape[0] // 2
    slots = 2 * sources
    count = slots * S
    steps = turned.shape[1] // BLOCK
    rows = ray_rows(received, sources)
    rows_v[...] = rows
    points = sample_rows(rows)
    for axis, coordinate in enumerate(points):
        factor[axis * CELLS : (axis + 1) * CELLS, :] = factors(coordinate)[0]
        points_v[axis : axis + 1, :] = coordinate
    points_v[3:8, :] = jnp.zeros((5, count), F32)
    leaving = fetch((rows_v, points_v), (rows_h, points_h), out_sems)
    total[...] = jnp.zeros_like(total)

    @pl.loop(0, steps, unroll=4)
    def _(step):
        row_base, col_base, _, _ = plane_axes(step)
        for lane in range(0, count, TILE):
            columns = factor[pl.ds(pl.multiple_of(col_base, CELLS), CELLS), lane : lane + TILE]
            acc = total[:, lane : lane + TILE]
            for part in range(BLOCK // TILE):
                tile = table_tile(factor, row_base, part, columns, lane)
                acc = acc + contract(plane_tile(turned, step, part), tile, 1, 0)
            total[:, lane : lane + TILE] = acc

    feats = total[...].astype(BF16)
    feats_v[...] = feats
    v1 = contract(first_t[...], feats, 1, 0)
    v1_v[...] = v1
    leaving += fetch((feats_v, v1_v), (feats_h, v1_h), out_sems, 2)
    h1 = (v1 * jax.nn.sigmoid(v1)).astype(BF16)
    v2 = contract(hidden_t[...], h1, 1, 0)
    v2_v[...] = v2
    leaving += fetch((v2_v,), (v2_h,), out_sems, 4)
    h2 = (v2 * jax.nn.sigmoid(v2)).astype(BF16)
    colors = jnp.tanh(contract(feature_t[...], h2, 1, 0))
    colors_v[0:LANES, :] = colors
    raw = contract(density_w[...].astype(BF16), h2, 1, 0)
    colors_v[LANES : LANES + 8, :] = jnp.broadcast_to(raw, (8, count))
    leaving += fetch((colors_v,), (colors_h,), out_sems, 5)
    depth = (jnp.maximum(raw, 0.0) + jnp.log1p(jnp.exp(-jnp.abs(raw)))) * STEP
    seg = jnp.zeros((LANES, slots), F32)
    front = jnp.zeros((1, slots), F32)
    for s in range(S):
        e = depth[:, s * slots : (s + 1) * slots]
        weight = jnp.exp(-front) * (1.0 - jnp.exp(-e))
        seg = seg + weight * colors[:, s * slots : (s + 1) * slots]
        front = front + e
    through = jnp.exp(-front)
    out[pl.ds(0, sources, stride=3), :] = seg[:, 0:sources].T
    out[pl.ds(1, sources, stride=3), :] = seg[:, sources:slots].T
    sub = iota((8, sources), 0)
    both = jnp.where(
        sub == 0, through[:, 0:sources], jnp.where(sub == 1, through[:, sources:slots], 0.0)
    )
    place = (iota((8, LANES), 0) == iota((8, LANES), 1)).astype(F32)
    out[pl.ds(2, sources, stride=3), :] = contract(both, place, 0, 0, EXACT)
    leaving += fetch((out,), (out_h,), out_sems, 6)
    for copy in leaving:
        copy.wait()


def plane_tile(turned, step, part):
    return turned[:, pl.ds(pl.multiple_of(step * BLOCK + part * TILE, TILE), TILE)]


def forward(received, turned, first_t, hidden_t, feature_t, density_w):
    sources = received.shape[0] // 2
    slots = 2 * sources
    count = slots * S
    channels, cells = turned.shape
    hidden = first_t.shape[0]
    saved = [
        ((3 * sources, LANES), F32),
        ((16, slots), F32),
        ((8, count), F32),
        ((channels, count), BF16),
        ((hidden, count), F32),
        ((hidden, count), F32),
        ((channels + 8, count), F32),
    ]
    return pl.pallas_call(
        forward_kernel,
        in_specs=[IN_VMEM] * 6,
        out_specs=[IN_HBM] * len(saved),
        out_shape=[pltpu.HBM(shape, kind) for shape, kind in saved],
        scratch_shapes=[pltpu.VMEM(shape, kind) for shape, kind in saved]
        + [
            pltpu.VMEM((3 * CELLS, count), F32),
            pltpu.VMEM((channels, count), F32),
            pltpu.SemaphoreType.DMA((len(saved),)),
        ],
        compiler_params=grant(16),
        cost_estimate=price(2 * cells * count * channels, 8 * 2**20),
        name="forward",
    )(received, turned, first_t, hidden_t, feature_t, density_w)


def slopes(points, planes, first_step, last_step, carried, begun=None):
    count = points.shape[1]
    channels = planes.shape[1]
    steps = last_step - first_step
    moved = len(carried)
    ending = begun is not None
    ins = list(carried) + ([begun] if ending else [])

    def slope_kernel(points_h, planes_h, *refs):
        given, refs = refs[: len(ins)], refs[len(ins) :]
        out, brought, refs = refs[0], refs[1 : 1 + moved], refs[1 + moved :]
        held, turned, points, factor, slope, total, plane_sems, in_sems = refs[:8]
        total = out if ending else total
        arriving = fetch((points_h,), (points,), in_sems)
        plane_copy = plane_copies(planes_h, held, plane_sems, first_step, last_step)
        arriving += fetch(given, brought + refs[8:], in_sems, 1)
        total[...] = jnp.zeros_like(total)
        arriving[0].wait()
        for axis in range(3):
            span = slice(axis * CELLS, (axis + 1) * CELLS)
            factor[span, :], slope[span, :] = factors(points[axis : axis + 1, :])

        @pl.loop(first_step, last_step, unroll=3)
        def _(step):
            plane_copy(step).wait()
            local = pl.ds(pl.multiple_of((step - first_step) * BLOCK, BLOCK), BLOCK)
            turned[...] = held[local, :].T.astype(BF16)
            row_base, col_base, first, second = plane_axes(step)
            for rows_ref, cols_ref, axis in ((slope, factor, first), (factor, slope, second)):
                base = pl.multiple_of(axis * LANES, LANES)
                for lane in range(0, count, TILE):
                    columns = cols_ref[
                        pl.ds(pl.multiple_of(col_base, CELLS), CELLS), lane : lane + TILE
                    ]
                    acc = total[pl.ds(base, LANES), lane : lane + TILE]
                    for part in range(BLOCK // TILE):
                        tile = table_tile(rows_ref, row_base, part, columns, lane)
                        acc = acc + contract(turned[:, part * TILE : (part + 1) * TILE], tile, 1, 0)
                    total[pl.ds(base, LANES), lane : lane + TILE] = acc

        for copy in arriving[1:]:
            copy.wait()
        if ending:
            out[...] = out[...] + refs[8][...].astype(F32)
        else:
            out[...] = total[...].astype(BF16)

    shape = (3 * channels, count)
    return pl.pallas_call(
        slope_kernel,
        in_specs=[IN_HBM] * (2 + len(ins)),
        out_specs=[IN_VMEM] * (1 + moved),
        out_shape=[jax.ShapeDtypeStruct(shape, F32) if ending else pltpu.HBM(shape, BF16)] + shapes(*carried),
        scratch_shapes=[
            pltpu.VMEM((steps * BLOCK, channels), F32),
            pltpu.VMEM((channels, BLOCK), BF16),
            pltpu.VMEM(points.shape, F32),
            pltpu.VMEM((3 * CELLS, count), F32),
            pltpu.VMEM((3 * CELLS, count), F32),
            pltpu.VMEM((8, 128) if ending else shape, F32),
            pltpu.SemaphoreType.DMA((steps,)),
            pltpu.SemaphoreType.DMA((1 + len(ins),)),
        ]
        + ([pltpu.VMEM(shape, BF16)] if ending else []),
        compiler_params=grant(16),
        cost_estimate=price(4 * steps * BLOCK * count * channels, 6 * 2**20),
        name="slopes",
    )(far(points), far(planes), *map(far, ins))


def rays_kernel(home, route, ranks, targets, ray_h, back_h, ray_out, back, grads, out_sems):
    bricks = home.shape[0] // 3
    rays = targets.shape[0]
    slot = [route[(2 + c) * bricks : (3 + c) * bricks, :] for c in range(2)]
    seg = select_rows(slot[0], home[pl.ds(0, bricks, stride=3), :], 1, 0) + select_rows(
        slot[1], home[pl.ds(1, bricks, stride=3), :], 1, 0
    )
    lane = iota((1, LANES), 1)
    through = home[pl.ds(2, bricks, stride=3), :]
    passing = jnp.sum(
        select_rows(slot[0], jnp.where(lane == 0, through, 0.0), 1, 0)
        + select_rows(slot[1], jnp.where(lane == 1, through, 0.0), 1, 0),
        axis=1,
        keepdims=True,
    )
    feature = [seg[k * rays : (k + 1) * rays] for k in range(K)]
    pass_k = [passing[k * rays : (k + 1) * rays] for k in range(K)]
    rank_cols = contract(eye(rays), ranks[...].astype(F32), 1, 1, EXACT)
    rank = [rank_cols[:, k : k + 1] for k in range(K)]
    ones = jnp.ones((rays, 1), F32)

    def seen(k, skip=None):
        product = ones
        for other in range(K):
            if other != k and other != skip:
                product = product * jnp.where(rank[other] < rank[k], pass_k[other], 1.0)
        return product

    transmit = [seen(k) for k in range(K)]
    ray = jnp.zeros_like(feature[0])
    for k in range(K):
        ray = ray + transmit[k] * feature[k]
    ray_out[...] = ray
    leaving = fetch((ray_out,), (ray_h,), out_sems)
    grad = ray - targets[...]
    pull = [jnp.sum(grad * feature[k], axis=1, keepdims=True) for k in range(K)]
    for k in range(K):
        grads[k * rays : (k + 1) * rays, 0:LANES] = transmit[k] * grad
        pass_grad = jnp.zeros((rays, 1), F32)
        for behind in range(K):
            if behind != k:
                pass_grad = pass_grad + jnp.where(
                    rank[k] < rank[behind], pull[behind] * seen(behind, k), 0.0
                )
        grads[k * rays : (k + 1) * rays, LANES : 2 * LANES] = jnp.broadcast_to(
            pass_grad, (rays, LANES)
        )
    spread = None
    for c in range(2):
        both = select_rows(route[c * bricks : (c + 1) * bricks, :], grads[...], 1, 0)
        back[pl.ds(c, bricks, stride=3), :] = both[:, 0:LANES]
        own = jnp.where(lane == c, both[:, LANES : 2 * LANES], 0.0)
        spread = own if spread is None else spread + own
    back[pl.ds(2, bricks, stride=3), :] = spread
    leaving += fetch((back,), (back_h,), out_sems, 1)
    for copy in leaving:
        copy.wait()


def rays_step(home, route, ranks, targets):
    return pl.pallas_call(
        rays_kernel,
        out_specs=[IN_HBM] * 2,
        out_shape=(pltpu.HBM(targets.shape, F32), pltpu.HBM(home.shape, F32)),
        scratch_shapes=[
            pltpu.VMEM(targets.shape, F32),
            pltpu.VMEM(home.shape, F32),
            pltpu.VMEM((route.shape[1], 2 * LANES), F32),
            pltpu.SemaphoreType.DMA((2,)),
        ],
        compiler_params=grant(4),
        name="rays",
    )(home, route, ranks, targets)


def backward_kernel(
    cot, slope_ref, colors_ref, v2_ref, feature_w, density_h, v1_h, hidden_h, feats_h, first_h, rows_h,
    pose_gh, feature_gh, density_gh, hidden_gh, first_gh, feat_cot_h,
    density_w, v1_ref, hidden_w, feats, first_w, rows_ref,
    feature_g, density_g, hidden_g, first_g, feat_cot,
    color_cot, pair, pose_g, in_sems, out_sems,
):
    arriving = fetch(
        (density_h, v1_h, hidden_h, feats_h, first_h, rows_h),
        (density_w, v1_ref, hidden_w, feats, first_w, rows_ref),
        in_sems,
    )
    sources = cot.shape[0] // 3
    slots = 2 * sources
    seg_cot = jnp.concatenate(
        [cot[pl.ds(slot, sources, stride=3), :].T for slot in range(2)], axis=1
    )
    turned = cot[pl.ds(2, sources, stride=3), :].T
    pass_cot = jnp.concatenate([turned[0:1], turned[1:2]], axis=1)
    raw = colors_ref[LANES : LANES + 1, :]
    depth = (jnp.maximum(raw, 0.0) + jnp.log1p(jnp.exp(-jnp.abs(raw)))) * STEP
    front = jnp.zeros((1, slots), F32)
    weights, kept, pulls = [], [], []
    for s in range(S):
        span = slice(s * slots, (s + 1) * slots)
        e = depth[:, span]
        reach = jnp.exp(-front)
        weight = reach * (1.0 - jnp.exp(-e))
        colors = colors_ref[0:LANES, span]
        pulls.append(jnp.sum(colors * seg_cot, axis=0, keepdims=True))
        color_cot[:, span] = (weight * seg_cot * (1.0 - colors * colors)).astype(BF16)
        weights.append(weight)
        kept.append(reach * jnp.exp(-e))
        front = front + e
    behind = pass_cot * jnp.exp(-front)
    depth_cot = [None] * S
    for s in reversed(range(S)):
        depth_cot[s] = pulls[s] * kept[s] - behind
        behind = behind + pulls[s] * weights[s]
    raw_cot = (jnp.concatenate(depth_cot, axis=1) * STEP * jax.nn.sigmoid(raw)).astype(BF16)

    v2 = v2_ref[...]
    gate2 = jax.nn.sigmoid(v2)
    h2 = (v2 * gate2).astype(BF16)
    color_c = color_cot[...]
    feature_g[...] = contract(h2, color_c, 1, 1).astype(BF16).astype(F32)
    density_g[...] = contract(raw_cot, h2, 1, 1).astype(BF16).astype(F32)
    for copy in arriving:
        copy.wait()
    leaving = fetch((feature_g, density_g), (feature_gh, density_gh), out_sems)
    wide = jnp.where(iota((8, 1), 0) == 0, density_w[...].astype(F32), 0.0).astype(BF16)
    wide_cot = jnp.where(iota((8, 1), 0) == 0, raw_cot.astype(F32), 0.0).astype(BF16)
    h2_cot = (
        contract(feature_w[...], color_c, 1, 0) + contract(wide.T, wide_cot, 1, 0)
    ).astype(BF16).astype(F32)
    v2_cot = (h2_cot * gate2 * (1.0 + v2 * (1.0 - gate2))).astype(BF16)
    v1 = v1_ref[...]
    gate1 = jax.nn.sigmoid(v1)
    h1 = (v1 * gate1).astype(BF16)
    hidden_g[...] = contract(h1, v2_cot, 1, 1).astype(BF16).astype(F32)
    leaving += fetch((hidden_g,), (hidden_gh,), out_sems, 2)
    h1_cot = contract(hidden_w[...], v2_cot, 1, 0).astype(BF16).astype(F32)
    v1_cot = (h1_cot * gate1 * (1.0 + v1 * (1.0 - gate1))).astype(BF16)
    first_g[...] = contract(feats[...], v1_cot, 1, 1).astype(BF16).astype(F32)
    f_cot = contract(first_w[...], v1_cot, 1, 0).astype(BF16).astype(F32)
    feat_cot[...] = f_cot.T.astype(BF16)
    leaving += fetch((first_g, feat_cot), (first_gh, feat_cot_h), out_sems, 3)

    pull = [
        jnp.sum(slope_ref[a * LANES : (a + 1) * LANES, :] * f_cot, axis=0, keepdims=True)
        for a in range(3)
    ]
    rows = rows_ref[...]
    shift = [jnp.zeros((1, slots), F32)] * 3
    turn = [jnp.zeros((1, slots), F32)] * 3
    for s in range(S):
        distance = rows[12:13] + (s + 0.5) * STEP
        place = [rows[6 + i : 7 + i] + distance * rows[9 + i : 10 + i] for i in range(3)]
        part = [pull[a][:, s * slots : (s + 1) * slots] for a in range(3)]
        twist = cross(place, part)
        for a in range(3):
            shift[a] = shift[a] + part[a]
            turn[a] = turn[a] + twist[a]
    sub = iota((8, slots), 0)
    grads = jnp.zeros((8, slots), F32)
    for a in range(3):
        grads = jnp.where(sub == a, turn[a], grads)
        grads = jnp.where(sub == 3 + a, shift[a], grads)
    cams = 2 * LANES
    picked = (iota((cams, slots), 0) == rows[13:14].astype(jnp.int32)).astype(F32)
    pose = contract(grads, picked, 1, 1, EXACT)
    for copy in range(2):
        for half in range(2):
            start = copy * 12 + half * 6
            pair[start : start + 6, :] = pose[0:6, half * LANES : (half + 1) * LANES]
    two = pair[...]
    for copy in range(pose_g.shape[0] // 24):
        pose_g[copy * 24 : (copy + 1) * 24, :] = two
    leaving += fetch((pose_g,), (pose_gh,), out_sems, 5)
    for copy in leaving:
        copy.wait()


def backward(cot, near, distant, copies):
    density_w, _, hidden_w, feats, first_w, _ = distant
    feature_w = near[-1]
    channels, count = feats.shape
    outs = [(w.shape, F32) for w in (feature_w, density_w, hidden_w, first_w)] + [((count, channels), BF16)]
    return pl.pallas_call(
        backward_kernel,
        in_specs=[IN_VMEM] * (len(near) + 1) + [IN_HBM] * len(distant),
        out_specs=[IN_HBM] * (1 + len(outs)),
        out_shape=[pltpu.HBM((12 * copies, LANES), F32)] + [pltpu.HBM(shape, kind) for shape, kind in outs],
        scratch_shapes=[pltpu.VMEM(x.shape, x.dtype) for x in distant]
        + [pltpu.VMEM(shape, kind) for shape, kind in outs]
        + [
            pltpu.VMEM((channels, count), BF16),
            pltpu.VMEM((24, LANES), F32),
            pltpu.VMEM((12 * copies, LANES), F32),
            pltpu.SemaphoreType.DMA((len(distant),)),
            pltpu.SemaphoreType.DMA((1 + len(outs),)),
        ],
        compiler_params=grant(16),
        name="backward",
    )(cot, *near, *map(far, distant))


def plane_grads(points, cot, cells):
    count = points.shape[1]
    channels = cot.shape[1]
    blocks = 2

    def plane_kernel(points, cot, out, factor):
        @pl.when(pl.program_id(0) == 0)
        def _():
            for axis in range(3):
                factor[axis * CELLS : (axis + 1) * CELLS, :] = factors(points[axis : axis + 1, :])[0]

        for block in range(blocks):
            row_base, col_base, _, _ = plane_axes(pl.program_id(0) * blocks + block)
            for part in range(BLOCK // TILE):
                acc = jnp.zeros((TILE, channels), F32)
                for lane in range(0, count, TILE):
                    columns = factor[pl.ds(pl.multiple_of(col_base, CELLS), CELLS), lane : lane + TILE]
                    tile = table_tile(factor, row_base, part, columns, lane)
                    acc = acc + contract(tile, cot[lane : lane + TILE, :], 1, 0)
                start = block * BLOCK + part * TILE
                out[start : start + TILE, :] = acc

    return pl.pallas_call(
        plane_kernel,
        grid=(cells // (blocks * BLOCK),),
        in_specs=[IN_VMEM, IN_VMEM],
        out_specs=pl.BlockSpec((blocks * BLOCK, channels), lambda step: (step, 0)),
        out_shape=pltpu.HBM((cells, channels), F32),
        scratch_shapes=[pltpu.VMEM((3 * CELLS, count), F32)],
        compiler_params=grant(8),
        cost_estimate=price(2 * cells * count * channels, cells * channels * 4),
        name="plane_grads",
    )(far(points), far(cot))


def exchange(rows, peers):
    wide = rows.reshape(peers, 1, rows.size // peers)
    moved = lax.all_to_all(wide, AXES, split_axis=0, concat_axis=0, tiled=True)
    return moved.reshape(rows.shape)


def add_kernel(parts, out):
    total = parts[0:24, :]
    for source in range(1, parts.shape[0] // 24):
        total = total + parts[source * 24 : (source + 1) * 24, :]
    total = total[0:12] + total[12:24]
    out[:, 0:LANES] = total[0:6]
    out[:, LANES : 2 * LANES] = total[6:12]


def add(parts, shape):
    return pl.pallas_call(
        add_kernel, out_shape=pltpu.HBM(shape, F32), compiler_params=grant(2), name="add"
    )(parts)


def per_device(
    anchors, directions, ray_start, camera_ids, brick_ids, brick_rank, targets,
    planes, first_weight, hidden_weight, feature_weight, density_weight, poses,
):
    bricks = lax.axis_size(AXES)
    cells = planes.shape[1]
    steps = cells // BLOCK
    ids, ranks = brick_ids.T, brick_rank.T
    outgoing = dispatch(
        anchors, directions, ray_start[None], camera_ids[None], ids, ranks, poses, bricks
    )
    received = exchange(outgoing, bricks)
    turned, first_t, hidden_t, feature_t, density_o, first_o, hidden_o, feature_o, route = prepare(
        planes[0], first_weight[0], hidden_weight[0, 0], feature_weight[0], density_weight, ids, bricks
    )
    sent, rows, points, feats, v1, v2, colors = forward(
        received, turned, first_t, hidden_t, feature_t, density_o
    )
    home = exchange(sent, bricks)
    begun, *ray_data = slopes(points, planes[0], 0, steps // 2, [route, ranks, targets])
    ray_feature, back = rays_step(home, *ray_data)
    cot = exchange(back, bricks)
    later_points, back = lax.optimization_barrier((points, back))
    near = slopes(
        later_points, planes[0], steps // 2, steps, [colors, v2, feature_o], begun
    )
    distant = [density_weight, v1, hidden_o, feats, first_o, rows]
    pose_part, feature_g, density_g, hidden_g, first_g, feat_cot = backward(
        cot, near, distant, bricks
    )
    pose_grad = add(exchange(pose_part, bricks), poses.shape)
    plane_grad = plane_grads(points, feat_cot, cells)
    return (
        ray_feature,
        plane_grad[None],
        first_g[None],
        hidden_g[None, None],
        feature_g[None],
        density_g,
        pose_grad,
    )


def solution(mesh):
    rays = P(AXES)
    in_specs = (
        P(None, AXES), P(None, AXES), rays, rays, P(AXES, None), P(AXES, None), P(AXES, None),
        P(AXES, None, None), P(AXES, None, None), P(AXES, None, None, None), P(AXES, None, None),
        P(AXES, None), P(),
    )
    out_specs = (
        P(AXES, None), P(AXES, None, None), P(AXES, None, None), P(AXES, None, None, None),
        P(AXES, None, None), P(AXES, None), P(),
    )
    return jax.shard_map(
        per_device, mesh=mesh, in_specs=in_specs, out_specs=out_specs, check_vma=False
    )
```

```python
import jax
import jax.numpy as jnp
from jax import lax
from jax.experimental import pallas as pl
from jax.experimental.pallas import tpu as pltpu
from jax.sharding import PartitionSpec as P

K = 4
S = 4
CELLS = 64
LANES = 128
STEP = 0.125
AXES = ("gx", "gy")
F32 = jnp.float32
BF16 = jnp.bfloat16
EXACT = lax.Precision.HIGHEST


def contract(left, right, left_dim, right_dim, precision=None):
    return lax.dot_general(
        left,
        right,
        (((left_dim,), (right_dim,)), ((), ())),
        precision=precision,
        preferred_element_type=F32,
    )


def iota(shape, dim):
    return lax.broadcasted_iota(jnp.int32, shape, dim)


def grant(mebibytes):
    return pltpu.CompilerParams(vmem_limit_bytes=mebibytes * 2**20)


def far(x):
    return pltpu.with_memory_space_constraint(x, pltpu.HBM)


def price(flops, moved):
    return pl.CostEstimate(flops=flops, bytes_accessed=moved, transcendentals=0)


def select_rows(onehot, values, left_dim, right_dim, parts=3):
    picked = onehot.astype(BF16)
    total = None
    rest = values
    for _ in range(parts):
        part = rest.astype(BF16)
        rest = rest - part.astype(F32)
        term = contract(picked, part, left_dim, right_dim)
        total = term if total is None else total + term
    return total


def with_onehot(values, onehot, left_dim, right_dim):
    picked = onehot.astype(BF16)
    total = None
    rest = values
    for _ in range(3):
        part = rest.astype(BF16)
        rest = rest - part.astype(F32)
        term = contract(part, picked, left_dim, right_dim)
        total = term if total is None else total + term
    return total


def eye(size):
    return (iota((size, size), 0) == iota((size, size), 1)).astype(F32)


def spread_of(rays):
    segs = rays * K
    spread = (iota((rays, segs), 0) == iota((rays, segs), 1) % rays).astype(F32)
    own = iota((K, segs), 0) == iota((K, segs), 1) // rays
    return spread, own


def segment_row(table, spread, own):
    four = contract(table[...].astype(F32).astype(BF16), spread.astype(BF16), 1, 0)
    return jnp.sum(jnp.where(own, four, 0.0), axis=0, keepdims=True)


def route_of(id_row, bricks):
    segs = id_row.shape[1]
    onehot = (iota((bricks, segs), 0) == id_row.astype(jnp.int32)).astype(F32)
    earlier = (iota((segs, segs), 0) < iota((segs, segs), 1)).astype(F32)
    before = contract(onehot.astype(BF16), earlier.astype(BF16), 1, 0)
    return [jnp.where((before > 0.5) == (slot == 1), onehot, 0.0) for slot in range(2)]


def cross(a, b):
    return (
        a[1] * b[2] - a[2] * b[1],
        a[2] * b[0] - a[0] * b[2],
        a[0] * b[1] - a[1] * b[0],
    )


def dispatch_kernel(anchors, directions, start, cameras, ids, ranks, poses, out, packed):
    bricks = out.shape[0] // 2
    rays = anchors.shape[1]
    spread, own = spread_of(rays)
    id_row = segment_row(ids, spread, own)
    picked = (iota((poses.shape[1], rays), 0) == cameras[...]).astype(F32)
    pose = with_onehot(poses[...], picked, 1, 0)
    turn = [pose[i : i + 1] for i in range(3)]
    anchor = [anchors[i : i + 1, :] for i in range(3)]
    direction = [directions[i : i + 1, :] for i in range(3)]
    turned = cross(turn, anchor)
    bent = cross(turn, direction)
    for i in range(3):
        packed[i : i + 1, :] = anchor[i] + turned[i] + pose[3 + i : 4 + i]
        packed[3 + i : 4 + i, :] = direction[i] + bent[i]
    packed[6:9, :] = anchors[...]
    packed[9:12, :] = directions[...]
    packed[12:13, :] = start[...]
    packed[13:14, :] = cameras[...].astype(F32)
    packed[14:16, :] = jnp.zeros((2, rays), F32)
    rank_row = segment_row(ranks, spread, own)
    values = with_onehot(packed[...], spread, 1, 0)
    values = values + jnp.where(iota((16, 1), 0) == 12, rank_row * (S * STEP), 0.0)
    for slot, taken in enumerate(route_of(id_row, bricks)):
        rows = select_rows(taken, values, 1, 1)
        both = jnp.concatenate([rows, jnp.zeros((bricks, LANES - 16), F32)], axis=1)
        out[pl.ds(slot, bricks, stride=2), :] = both


def dispatch(anchors, directions, start, cameras, ids, ranks, poses, bricks):
    return pl.pallas_call(
        dispatch_kernel,
        out_shape=jax.ShapeDtypeStruct((2 * bricks, LANES), F32),
        scratch_shapes=[pltpu.VMEM((16, anchors.shape[1]), F32)],
        compiler_params=grant(2),
        name="dispatch",
    )(*map(far, (anchors, directions, start, cameras, ids, ranks, poses)))


def ray_rows(received, sources):
    return jnp.concatenate(
        [received[pl.ds(slot, sources, stride=2), :].T[0:16] for slot in range(2)], axis=1
    )


def sample_rows(rows):
    distance = [rows[12:13] + (s + 0.5) * STEP for s in range(S)]
    return [
        jnp.concatenate(
            [rows[i : i + 1] + distance[s] * rows[3 + i : 4 + i] for s in range(S)], axis=1
        )
        for i in range(3)
    ]


def factors(coordinate):
    count = coordinate.shape[1]
    scaled = coordinate * CELLS
    floor_c = jnp.floor(scaled)
    fraction = scaled - floor_c
    weight = fraction * fraction * (3.0 - 2.0 * fraction)
    slope = (6.0 * CELLS) * fraction * (1.0 - fraction)
    low = lax.bitwise_and(floor_c.astype(jnp.int32), CELLS - 1)
    high = lax.bitwise_and(low + 1, CELLS - 1)
    cell = iota((CELLS, count), 0)
    at_low = cell == low
    at_high = cell == high
    value = jnp.where(at_low, 1.0 - weight, 0.0) + jnp.where(at_high, weight, 0.0)
    change = jnp.where(at_high, slope, 0.0) - jnp.where(at_low, slope, 0.0)
    return value, change


BLOCK = 1024
TILE = 256


def plane_axes(step):
    plane = step // (CELLS * CELLS // BLOCK)
    first = plane // 2
    second = min(plane + 1, 2) if isinstance(step, int) else jnp.minimum(plane + 1, 2)
    start = (step % (CELLS * CELLS // BLOCK)) * (BLOCK // CELLS)
    return first * CELLS + start, second * CELLS, first, second


def table_tile(rows_ref, row_base, part, columns, lane):
    pieces = []
    for i in range(TILE // CELLS):
        row = rows_ref[pl.ds(row_base + part * (TILE // CELLS) + i, 1), lane : lane + TILE]
        pieces.append((row * columns).astype(BF16))
    return jnp.concatenate(pieces, axis=0)


IN_HBM = pl.BlockSpec(memory_space=pltpu.HBM)
IN_VMEM = pl.BlockSpec(memory_space=pltpu.VMEM)


def shapes(*arrays):
    return [jax.ShapeDtypeStruct(x.shape, x.dtype) for x in arrays]


def fetch(sources, places, sems, first=0):
    copies = [
        pltpu.make_async_copy(source, place, sems.at[first + i])
        for i, (source, place) in enumerate(zip(sources, places))
    ]
    for copy in copies:
        copy.start()
    return copies


def plane_copies(planes, held, sems, first_step, last_step):
    def copy(step):
        start = pl.multiple_of(step * BLOCK, BLOCK)
        local = pl.multiple_of((step - first_step) * BLOCK, BLOCK)
        return pltpu.make_async_copy(
            planes.at[pl.ds(start, BLOCK), :], held.at[pl.ds(local, BLOCK), :], sems.at[step - first_step]
        )

    for step in range(first_step, last_step):
        copy(step).start()
    return copy


def prepare_kernel(
    planes, first_h, hidden_h, feature_h, density_h, ids_h,
    turned, first_t, hidden_t, feature_t, density_w, first_oh, hidden_oh, feature_oh, route_h,
    held, first_w, hidden_w, feature_w, ids, first_o, hidden_o, feature_o, route, plane_sems, in_sems, out_sems,
):
    steps = planes.shape[0] // BLOCK
    arriving = fetch(
        (ids_h, first_h, hidden_h, feature_h, density_h), (ids, first_w, hidden_w, feature_w, density_w), in_sems
    )
    plane_copy = plane_copies(planes, held, plane_sems, 0, steps)
    for copy in arriving:
        copy.wait()
    for source, plain, flipped in (
        (first_w, first_o, first_t),
        (hidden_w, hidden_o, hidden_t),
        (feature_w, feature_o, feature_t),
    ):
        plain[...] = source[...].astype(BF16)
        flipped[...] = source[...].T.astype(BF16)
    bricks = route.shape[0] // 4
    spread, own = spread_of(ids.shape[1])
    for slot, taken in enumerate(route_of(segment_row(ids, spread, own), bricks)):
        route[slot * bricks : (slot + 1) * bricks, :] = taken.astype(BF16)
        route[(2 + slot) * bricks : (3 + slot) * bricks, :] = taken.T.astype(BF16)
    leaving = fetch((first_o, hidden_o, feature_o, route), (first_oh, hidden_oh, feature_oh, route_h), out_sems)

    @pl.loop(0, steps)
    def _(step):
        plane_copy(step).wait()
        span = pl.ds(pl.multiple_of(step * BLOCK, BLOCK), BLOCK)
        turned[:, span] = held[span, :].T.astype(BF16)

    for copy in leaving:
        copy.wait()


def prepare(planes, first_w, hidden_w, feature_w, density_w, ids, bricks):
    cells, channels = planes.shape
    flips = [jax.ShapeDtypeStruct(w.shape[::-1], BF16) for w in (first_w, hidden_w, feature_w)]
    plains = [pltpu.HBM(w.shape, BF16) for w in (first_w, hidden_w, feature_w)]
    return pl.pallas_call(
        prepare_kernel,
        in_specs=[IN_HBM] * 6,
        out_specs=[IN_VMEM] * 5 + [IN_HBM] * 4,
        out_shape=[jax.ShapeDtypeStruct((channels, cells), BF16)]
        + flips
        + shapes(density_w)
        + plains
        + [pltpu.HBM((4 * bricks, ids.shape[1] * K), BF16)],
        scratch_shapes=[pltpu.VMEM((cells, channels), F32)]
        + [pltpu.VMEM(x.shape, x.dtype) for x in (first_w, hidden_w, feature_w, ids)]
        + [pltpu.VMEM(w.shape, BF16) for w in (first_w, hidden_w, feature_w)]
        + [
            pltpu.VMEM((4 * bricks, ids.shape[1] * K), BF16),
            pltpu.SemaphoreType.DMA((cells // BLOCK,)),
            pltpu.SemaphoreType.DMA((5,)),
            pltpu.SemaphoreType.DMA((4,)),
        ],
        compiler_params=grant(16),
        cost_estimate=price(0, 10 * 2**20),
        name="prepare",
    )(*map(far, (planes, first_w, hidden_w, feature_w, density_w, ids)))


def forward_kernel(
    received, turned, first_t, hidden_t, feature_t, density_w,
    out_h, rows_h, points_h, feats_h, v1_h, v2_h, colors_h, turned_h,
    out, rows_v, points_v, feats_v, v1_v, v2_v, colors_v,
    factor, total, out_sems,
):
    sources = received.shape[0] // 2
    slots = 2 * sources
    count = slots * S
    steps = turned.shape[1] // BLOCK
    leaving = fetch((turned,), (turned_h,), out_sems, 7)
    rows = ray_rows(received, sources)
    rows_v[...] = rows
    points = sample_rows(rows)
    for axis, coordinate in enumerate(points):
        factor[axis * CELLS : (axis + 1) * CELLS, :] = factors(coordinate)[0]
        points_v[axis : axis + 1, :] = coordinate
    points_v[3:8, :] = jnp.zeros((5, count), F32)
    leaving += fetch((rows_v, points_v), (rows_h, points_h), out_sems)
    total[...] = jnp.zeros_like(total)

    for step in range(steps):
        row_base, col_base, _, _ = plane_axes(step)
        for lane in range(0, count, TILE):
            columns = factor[col_base : col_base + CELLS, lane : lane + TILE]
            acc = total[:, lane : lane + TILE]
            for part in range(BLOCK // TILE):
                tile = table_tile(factor, row_base, part, columns, lane)
                start = step * BLOCK + part * TILE
                acc = acc + contract(turned[:, start : start + TILE], tile, 1, 0)
            total[:, lane : lane + TILE] = acc

    feats = total[...].astype(BF16)
    feats_v[...] = feats
    v1 = contract(first_t[...], feats, 1, 0)
    v1_v[...] = v1
    leaving += fetch((feats_v, v1_v), (feats_h, v1_h), out_sems, 2)
    h1 = (v1 * jax.nn.sigmoid(v1)).astype(BF16)
    v2 = contract(hidden_t[...], h1, 1, 0)
    v2_v[...] = v2
    leaving += fetch((v2_v,), (v2_h,), out_sems, 4)
    h2 = (v2 * jax.nn.sigmoid(v2)).astype(BF16)
    colors = jnp.tanh(contract(feature_t[...], h2, 1, 0))
    colors_v[0:LANES, :] = colors
    raw = contract(density_w[...].astype(BF16), h2, 1, 0)
    colors_v[LANES : LANES + 8, :] = jnp.broadcast_to(raw, (8, count))
    leaving += fetch((colors_v,), (colors_h,), out_sems, 5)
    depth = (jnp.maximum(raw, 0.0) + jnp.log1p(jnp.exp(-jnp.abs(raw)))) * STEP
    seg = jnp.zeros((LANES, slots), F32)
    front = jnp.zeros((1, slots), F32)
    for s in range(S):
        e = depth[:, s * slots : (s + 1) * slots]
        weight = jnp.exp(-front) * (1.0 - jnp.exp(-e))
        seg = seg + weight * colors[:, s * slots : (s + 1) * slots]
        front = front + e
    through = jnp.exp(-front)
    out[pl.ds(0, sources, stride=3), :] = seg[:, 0:sources].T
    out[pl.ds(1, sources, stride=3), :] = seg[:, sources:slots].T
    sub = iota((LANES, sources), 0)
    both = jnp.where(
        sub == 0, through[:, 0:sources], jnp.where(sub == 1, through[:, sources:slots], 0.0)
    )
    out[pl.ds(2, sources, stride=3), :] = both.T
    leaving += fetch((out,), (out_h,), out_sems, 6)
    for copy in leaving:
        copy.wait()


def forward(received, turned, first_t, hidden_t, feature_t, density_w):
    sources = received.shape[0] // 2
    slots = 2 * sources
    count = slots * S
    channels, cells = turned.shape
    hidden = first_t.shape[0]
    saved = [
        ((3 * sources, LANES), F32),
        ((16, slots), F32),
        ((8, count), F32),
        ((channels, count), BF16),
        ((hidden, count), F32),
        ((hidden, count), F32),
        ((channels + 8, count), F32),
    ]
    return pl.pallas_call(
        forward_kernel,
        in_specs=[IN_VMEM] * 6,
        out_specs=[IN_HBM] * (len(saved) + 1),
        out_shape=[pltpu.HBM(shape, kind) for shape, kind in saved + [(turned.shape, BF16)]],
        scratch_shapes=[pltpu.VMEM(shape, kind) for shape, kind in saved]
        + [
            pltpu.VMEM((3 * CELLS, count), F32),
            pltpu.VMEM((channels, count), F32),
            pltpu.SemaphoreType.DMA((len(saved) + 1,)),
        ],
        compiler_params=grant(16),
        cost_estimate=price(2 * cells * count * channels, 8 * 2**20),
        name="forward",
    )(received, turned, first_t, hidden_t, feature_t, density_w)


def slopes(points, planes_t, first_step, last_step, carried, begun=None):
    count = points.shape[1]
    channels = planes_t.shape[0]
    steps = last_step - first_step
    moved = len(carried)
    ending = begun is not None
    ins = list(carried) + ([begun] if ending else [])

    def slope_kernel(points_h, planes_h, *refs):
        given, refs = refs[: len(ins)], refs[len(ins) :]
        out, brought, refs = refs[0], refs[1 : 1 + moved], refs[1 + moved :]
        turned, points, factor, slope, total, plane_sems, in_sems = refs[:7]
        if ending:
            total = out
        else:
            rounded, out_sems = refs[7:]
        arriving = fetch((points_h,), (points,), in_sems)
        blocks = [
            pltpu.make_async_copy(
                planes_h.at[:, (first_step + step) * BLOCK : (first_step + step + 1) * BLOCK],
                turned.at[:, step * BLOCK : (step + 1) * BLOCK],
                plane_sems.at[step],
            )
            for step in range(steps)
        ]
        for copy in blocks:
            copy.start()
        arriving += fetch(given, brought + (refs[7:] if ending else ()), in_sems, 1)
        total[...] = jnp.zeros_like(total)
        arriving[0].wait()
        for axis in range(3):
            span = slice(axis * CELLS, (axis + 1) * CELLS)
            factor[span, :], slope[span, :] = factors(points[axis : axis + 1, :])

        leaving = []
        for step in range(steps):
            blocks[step].wait()
            row_base, col_base, first, second = plane_axes(first_step + step)
            for rows_ref, cols_ref, axis in ((slope, factor, first), (factor, slope, second)):
                rows = slice(axis * LANES, (axis + 1) * LANES)
                for lane in range(0, count, TILE):
                    here = slice(lane, lane + TILE)
                    columns = cols_ref[col_base : col_base + CELLS, here]
                    acc = total[rows, here]
                    for part in range(BLOCK // TILE):
                        tile = table_tile(rows_ref, row_base, part, columns, lane)
                        start = step * BLOCK + part * TILE
                        acc = acc + contract(turned[:, start : start + TILE], tile, 1, 0)
                    total[rows, here] = acc
        if ending:
            for copy in arriving[1:]:
                copy.wait()
            out[...] = out[...] + refs[7][...].astype(F32)
        else:
            for axis in range(3):
                rows = slice(axis * LANES, (axis + 1) * LANES)
                rounded[rows, :] = total[rows, :].astype(BF16)
                copy = pltpu.make_async_copy(rounded.at[rows, :], out.at[rows, :], out_sems.at[axis])
                copy.start()
                leaving.append(copy)
            for copy in arriving[1:] + leaving:
                copy.wait()

    shape = (3 * channels, count)
    return pl.pallas_call(
        slope_kernel,
        in_specs=[IN_HBM] * (2 + len(ins)),
        out_specs=[IN_VMEM if ending else IN_HBM] + [IN_VMEM] * moved,
        out_shape=[jax.ShapeDtypeStruct(shape, F32) if ending else pltpu.HBM(shape, BF16)] + shapes(*carried),
        scratch_shapes=[
            pltpu.VMEM((channels, steps * BLOCK), BF16),
            pltpu.VMEM(points.shape, F32),
            pltpu.VMEM((3 * CELLS, count), F32),
            pltpu.VMEM((3 * CELLS, count), F32),
            pltpu.VMEM((8, 128) if ending else shape, F32),
            pltpu.SemaphoreType.DMA((steps,)),
            pltpu.SemaphoreType.DMA((1 + len(ins),)),
        ]
        + [pltpu.VMEM(shape, BF16)]
        + ([] if ending else [pltpu.SemaphoreType.DMA((3,))]),
        compiler_params=grant(16),
        cost_estimate=price(4 * steps * BLOCK * count * channels, 6 * 2**20),
        name="slopes",
    )(far(points), far(planes_t), *map(far, ins))


def rays_kernel(home, route, ranks, targets, ray_h, back_h, ray_out, back, grads, out_sems):
    bricks = home.shape[0] // 3
    rays = targets.shape[0]
    slot = [route[(2 + c) * bricks : (3 + c) * bricks, :] for c in range(2)]
    seg = select_rows(slot[0], home[pl.ds(0, bricks, stride=3), :], 1, 0) + select_rows(
        slot[1], home[pl.ds(1, bricks, stride=3), :], 1, 0
    )
    lane = iota((1, LANES), 1)
    through = home[pl.ds(2, bricks, stride=3), :]
    passing = jnp.sum(
        select_rows(slot[0], jnp.where(lane == 0, through, 0.0), 1, 0)
        + select_rows(slot[1], jnp.where(lane == 1, through, 0.0), 1, 0),
        axis=1,
        keepdims=True,
    )
    feature = [seg[k * rays : (k + 1) * rays] for k in range(K)]
    pass_k = [passing[k * rays : (k + 1) * rays] for k in range(K)]
    rank_cols = contract(eye(rays), ranks[...].astype(F32), 1, 1, EXACT)
    rank = [rank_cols[:, k : k + 1] for k in range(K)]
    ones = jnp.ones((rays, 1), F32)

    def seen(k, skip=None):
        product = ones
        for other in range(K):
            if other != k and other != skip:
                product = product * jnp.where(rank[other] < rank[k], pass_k[other], 1.0)
        return product

    transmit = [seen(k) for k in range(K)]
    ray = jnp.zeros_like(feature[0])
    for k in range(K):
        ray = ray + transmit[k] * feature[k]
    ray_out[...] = ray
    leaving = fetch((ray_out,), (ray_h,), out_sems)
    grad = ray - targets[...]
    pull = [jnp.sum(grad * feature[k], axis=1, keepdims=True) for k in range(K)]
    for k in range(K):
        grads[k * rays : (k + 1) * rays, 0:LANES] = transmit[k] * grad
        pass_grad = jnp.zeros((rays, 1), F32)
        for behind in range(K):
            if behind != k:
                pass_grad = pass_grad + jnp.where(
                    rank[k] < rank[behind], pull[behind] * seen(behind, k), 0.0
                )
        grads[k * rays : (k + 1) * rays, LANES : 2 * LANES] = jnp.broadcast_to(
            pass_grad, (rays, LANES)
        )
    spread = None
    for c in range(2):
        both = select_rows(route[c * bricks : (c + 1) * bricks, :], grads[...], 1, 0)
        back[pl.ds(c, bricks, stride=3), :] = both[:, 0:LANES]
        own = jnp.where(lane == c, both[:, LANES : 2 * LANES], 0.0)
        spread = own if spread is None else spread + own
    back[pl.ds(2, bricks, stride=3), :] = spread
    leaving += fetch((back,), (back_h,), out_sems, 1)
    for copy in leaving:
        copy.wait()


def rays_step(home, route, ranks, targets):
    return pl.pallas_call(
        rays_kernel,
        out_specs=[IN_HBM] * 2,
        out_shape=(pltpu.HBM(targets.shape, F32), pltpu.HBM(home.shape, F32)),
        scratch_shapes=[
            pltpu.VMEM(targets.shape, F32),
            pltpu.VMEM(home.shape, F32),
            pltpu.VMEM((route.shape[1], 2 * LANES), F32),
            pltpu.SemaphoreType.DMA((2,)),
        ],
        compiler_params=grant(4),
        name="rays",
    )(home, route, ranks, targets)


def backward_kernel(
    cot, slope_ref, colors_ref, v2_ref, feature_w, density_h, v1_h, hidden_h, feats_h, first_h, rows_h,
    pose_gh, feature_gh, density_gh, hidden_gh, first_gh, feat_cot_h,
    density_w, v1_ref, hidden_w, feats, first_w, rows_ref,
    feature_g, density_g, hidden_g, first_g, feat_cot,
    color_cot, pair, pose_g, in_sems, out_sems,
):
    arriving = fetch(
        (density_h, v1_h, hidden_h, feats_h, first_h, rows_h),
        (density_w, v1_ref, hidden_w, feats, first_w, rows_ref),
        in_sems,
    )
    sources = cot.shape[0] // 3
    slots = 2 * sources
    seg_cot = jnp.concatenate(
        [cot[pl.ds(slot, sources, stride=3), :].T for slot in range(2)], axis=1
    )
    turned = cot[pl.ds(2, sources, stride=3), :].T
    pass_cot = jnp.concatenate([turned[0:1], turned[1:2]], axis=1)
    raw = colors_ref[LANES : LANES + 1, :]
    depth = (jnp.maximum(raw, 0.0) + jnp.log1p(jnp.exp(-jnp.abs(raw)))) * STEP
    front = jnp.zeros((1, slots), F32)
    weights, kept, pulls = [], [], []
    for s in range(S):
        span = slice(s * slots, (s + 1) * slots)
        e = depth[:, span]
        reach = jnp.exp(-front)
        weight = reach * (1.0 - jnp.exp(-e))
        colors = colors_ref[0:LANES, span]
        pulls.append(jnp.sum(colors * seg_cot, axis=0, keepdims=True))
        color_cot[:, span] = (weight * seg_cot * (1.0 - colors * colors)).astype(BF16)
        weights.append(weight)
        kept.append(reach * jnp.exp(-e))
        front = front + e
    behind = pass_cot * jnp.exp(-front)
    depth_cot = [None] * S
    for s in reversed(range(S)):
        depth_cot[s] = pulls[s] * kept[s] - behind
        behind = behind + pulls[s] * weights[s]
    raw_cot = (jnp.concatenate(depth_cot, axis=1) * STEP * jax.nn.sigmoid(raw)).astype(BF16)

    v2 = v2_ref[...]
    gate2 = jax.nn.sigmoid(v2)
    h2 = (v2 * gate2).astype(BF16)
    color_c = color_cot[...]
    feature_g[...] = contract(h2, color_c, 1, 1).astype(BF16).astype(F32)
    density_g[...] = contract(raw_cot, h2, 1, 1).astype(BF16).astype(F32)
    for copy in arriving:
        copy.wait()
    leaving = fetch((feature_g, density_g), (feature_gh, density_gh), out_sems)
    wide = jnp.where(iota((8, 1), 0) == 0, density_w[...].astype(F32), 0.0).astype(BF16)
    wide_cot = jnp.where(iota((8, 1), 0) == 0, raw_cot.astype(F32), 0.0).astype(BF16)
    h2_cot = (
        contract(feature_w[...], color_c, 1, 0) + contract(wide.T, wide_cot, 1, 0)
    ).astype(BF16).astype(F32)
    v2_cot = (h2_cot * gate2 * (1.0 + v2 * (1.0 - gate2))).astype(BF16)
    v1 = v1_ref[...]
    gate1 = jax.nn.sigmoid(v1)
    h1 = (v1 * gate1).astype(BF16)
    hidden_g[...] = contract(h1, v2_cot, 1, 1).astype(BF16).astype(F32)
    leaving += fetch((hidden_g,), (hidden_gh,), out_sems, 2)
    h1_cot = contract(hidden_w[...], v2_cot, 1, 0).astype(BF16).astype(F32)
    v1_cot = (h1_cot * gate1 * (1.0 + v1 * (1.0 - gate1))).astype(BF16)
    first_g[...] = contract(feats[...], v1_cot, 1, 1).astype(BF16).astype(F32)
    f_cot = contract(first_w[...], v1_cot, 1, 0).astype(BF16).astype(F32)
    feat_cot[...] = f_cot.T.astype(BF16)
    leaving += fetch((first_g, feat_cot), (first_gh, feat_cot_h), out_sems, 3)

    pull = [
        jnp.sum(slope_ref[a * LANES : (a + 1) * LANES, :] * f_cot, axis=0, keepdims=True)
        for a in range(3)
    ]
    rows = rows_ref[...]
    shift = [jnp.zeros((1, slots), F32)] * 3
    turn = [jnp.zeros((1, slots), F32)] * 3
    for s in range(S):
        distance = rows[12:13] + (s + 0.5) * STEP
        place = [rows[6 + i : 7 + i] + distance * rows[9 + i : 10 + i] for i in range(3)]
        part = [pull[a][:, s * slots : (s + 1) * slots] for a in range(3)]
        twist = cross(place, part)
        for a in range(3):
            shift[a] = shift[a] + part[a]
            turn[a] = turn[a] + twist[a]
    sub = iota((8, slots), 0)
    grads = jnp.zeros((8, slots), F32)
    for a in range(3):
        grads = jnp.where(sub == a, turn[a], grads)
        grads = jnp.where(sub == 3 + a, shift[a], grads)
    cams = 2 * LANES
    picked = (iota((cams, slots), 0) == rows[13:14].astype(jnp.int32)).astype(F32)
    pose = with_onehot(grads, picked, 1, 1)
    for copy in range(2):
        for half in range(2):
            start = copy * 12 + half * 6
            pair[start : start + 6, :] = pose[0:6, half * LANES : (half + 1) * LANES]
    two = pair[...]
    for copy in range(pose_g.shape[0] // 24):
        pose_g[copy * 24 : (copy + 1) * 24, :] = two
    leaving += fetch((pose_g,), (pose_gh,), out_sems, 5)
    for copy in leaving:
        copy.wait()


def backward(cot, near, distant, copies):
    density_w, _, hidden_w, feats, first_w, _ = distant
    feature_w = near[-1]
    channels, count = feats.shape
    outs = [(w.shape, F32) for w in (feature_w, density_w, hidden_w, first_w)] + [((count, channels), BF16)]
    return pl.pallas_call(
        backward_kernel,
        in_specs=[IN_VMEM] * (len(near) + 1) + [IN_HBM] * len(distant),
        out_specs=[IN_HBM] * (1 + len(outs)),
        out_shape=[pltpu.HBM((12 * copies, LANES), F32)] + [pltpu.HBM(shape, kind) for shape, kind in outs],
        scratch_shapes=[pltpu.VMEM(x.shape, x.dtype) for x in distant]
        + [pltpu.VMEM(shape, kind) for shape, kind in outs]
        + [
            pltpu.VMEM((channels, count), BF16),
            pltpu.VMEM((24, LANES), F32),
            pltpu.VMEM((12 * copies, LANES), F32),
            pltpu.SemaphoreType.DMA((len(distant),)),
            pltpu.SemaphoreType.DMA((1 + len(outs),)),
        ],
        compiler_params=grant(16),
        name="backward",
    )(cot, *near, *map(far, distant))


def plane_grads(points, cot, cells):
    count = points.shape[1]
    channels = cot.shape[1]
    blocks = 2

    def plane_kernel(points, cot, out, factor):
        @pl.when(pl.program_id(0) == 0)
        def _():
            for axis in range(3):
                factor[axis * CELLS : (axis + 1) * CELLS, :] = factors(points[axis : axis + 1, :])[0]

        for block in range(blocks):
            row_base, col_base, _, _ = plane_axes(pl.program_id(0) * blocks + block)
            for part in range(BLOCK // TILE):
                acc = jnp.zeros((TILE, channels), F32)
                for lane in range(0, count, TILE):
                    columns = factor[pl.ds(pl.multiple_of(col_base, CELLS), CELLS), lane : lane + TILE]
                    tile = table_tile(factor, row_base, part, columns, lane)
                    acc = acc + contract(tile, cot[lane : lane + TILE, :], 1, 0)
                start = block * BLOCK + part * TILE
                out[start : start + TILE, :] = acc

    return pl.pallas_call(
        plane_kernel,
        grid=(cells // (blocks * BLOCK),),
        in_specs=[IN_VMEM, IN_VMEM],
        out_specs=pl.BlockSpec((blocks * BLOCK, channels), lambda step: (step, 0)),
        out_shape=pltpu.HBM((cells, channels), F32),
        scratch_shapes=[pltpu.VMEM((3 * CELLS, count), F32)],
        compiler_params=grant(8),
        cost_estimate=price(2 * cells * count * channels, cells * channels * 4),
        name="plane_grads",
    )(far(points), far(cot))


def exchange(rows, peers):
    wide = rows.reshape(peers, 1, rows.size // peers)
    moved = lax.all_to_all(wide, AXES, split_axis=0, concat_axis=0, tiled=True)
    return moved.reshape(rows.shape)


def add_kernel(parts, out):
    total = parts[0:24, :]
    for source in range(1, parts.shape[0] // 24):
        total = total + parts[source * 24 : (source + 1) * 24, :]
    total = total[0:12] + total[12:24]
    out[:, 0:LANES] = total[0:6]
    out[:, LANES : 2 * LANES] = total[6:12]


def add(parts, shape):
    return pl.pallas_call(
        add_kernel, out_shape=pltpu.HBM(shape, F32), compiler_params=grant(2), name="add"
    )(parts)


def per_device(
    anchors, directions, ray_start, camera_ids, brick_ids, brick_rank, targets,
    planes, first_weight, hidden_weight, feature_weight, density_weight, poses,
):
    bricks = lax.axis_size(AXES)
    cells = planes.shape[1]
    steps = cells // BLOCK
    ids, ranks = brick_ids.T, brick_rank.T
    outgoing = dispatch(
        anchors, directions, ray_start[None], camera_ids[None], ids, ranks, poses, bricks
    )
    received = exchange(outgoing, bricks)
    turned, first_t, hidden_t, feature_t, density_o, first_o, hidden_o, feature_o, route = prepare(
        planes[0], first_weight[0], hidden_weight[0, 0], feature_weight[0], density_weight, ids, bricks
    )
    sent, rows, points, feats, v1, v2, colors, turned_far = forward(
        received, turned, first_t, hidden_t, feature_t, density_o
    )
    home = exchange(sent, bricks)
    begun, *ray_data = slopes(points, turned_far, 0, steps // 2, [route, ranks, targets])
    ray_feature, back = rays_step(home, *ray_data)
    cot = exchange(back, bricks)
    later_points, back = lax.optimization_barrier((points, back))
    near = slopes(
        later_points, turned_far, steps // 2, steps, [colors, v2, feature_o], begun
    )
    distant = [density_weight, v1, hidden_o, feats, first_o, rows]
    pose_part, feature_g, density_g, hidden_g, first_g, feat_cot = backward(
        cot, near, distant, bricks
    )
    pose_grad = add(exchange(pose_part, bricks), poses.shape)
    plane_grad = plane_grads(points, feat_cot, cells)
    return (
        ray_feature,
        plane_grad[None],
        first_g[None],
        hidden_g[None, None],
        feature_g[None],
        density_g,
        pose_grad,
    )


def solution(mesh):
    rays = P(AXES)
    in_specs = (
        P(None, AXES), P(None, AXES), rays, rays, P(AXES, None), P(AXES, None), P(AXES, None),
        P(AXES, None, None), P(AXES, None, None), P(AXES, None, None, None), P(AXES, None, None),
        P(AXES, None), P(),
    )
    out_specs = (
        P(AXES, None), P(AXES, None, None), P(AXES, None, None), P(AXES, None, None, None),
        P(AXES, None, None), P(AXES, None), P(),
    )
    return jax.shard_map(
        per_device, mesh=mesh, in_specs=in_specs, out_specs=out_specs, check_vma=False
    )
```

```python
import jax
import jax.numpy as jnp
from jax import lax
from jax.experimental import pallas as pl
from jax.experimental.pallas import tpu as pltpu
from jax.sharding import PartitionSpec as P

K = 4
S = 4
CELLS = 64
LANES = 128
STEP = 0.125
AXES = ("gx", "gy")
F32 = jnp.float32
BF16 = jnp.bfloat16
EXACT = lax.Precision.HIGHEST


def contract(left, right, left_dim, right_dim, precision=None):
    return lax.dot_general(
        left,
        right,
        (((left_dim,), (right_dim,)), ((), ())),
        precision=precision,
        preferred_element_type=F32,
    )


def iota(shape, dim):
    return lax.broadcasted_iota(jnp.int32, shape, dim)


def grant(mebibytes):
    return pltpu.CompilerParams(vmem_limit_bytes=mebibytes * 2**20)


def far(x):
    return pltpu.with_memory_space_constraint(x, pltpu.HBM)


def price(flops, moved):
    return pl.CostEstimate(flops=flops, bytes_accessed=moved, transcendentals=0)


def select_rows(onehot, values, left_dim, right_dim, parts=3):
    picked = onehot.astype(BF16)
    total = None
    rest = values
    for _ in range(parts):
        part = rest.astype(BF16)
        rest = rest - part.astype(F32)
        term = contract(picked, part, left_dim, right_dim)
        total = term if total is None else total + term
    return total


def with_onehot(values, onehot, left_dim, right_dim):
    picked = onehot.astype(BF16)
    total = None
    rest = values
    for _ in range(3):
        part = rest.astype(BF16)
        rest = rest - part.astype(F32)
        term = contract(part, picked, left_dim, right_dim)
        total = term if total is None else total + term
    return total


def eye(size):
    return (iota((size, size), 0) == iota((size, size), 1)).astype(F32)


def spread_of(rays):
    segs = rays * K
    spread = (iota((rays, segs), 0) == iota((rays, segs), 1) % rays).astype(F32)
    own = iota((K, segs), 0) == iota((K, segs), 1) // rays
    return spread, own


def segment_row(table, spread, own):
    four = contract(table[...].astype(F32).astype(BF16), spread.astype(BF16), 1, 0)
    return jnp.sum(jnp.where(own, four, 0.0), axis=0, keepdims=True)


def route_of(id_row, bricks):
    segs = id_row.shape[1]
    onehot = (iota((bricks, segs), 0) == id_row.astype(jnp.int32)).astype(F32)
    earlier = (iota((segs, segs), 0) < iota((segs, segs), 1)).astype(F32)
    before = contract(onehot.astype(BF16), earlier.astype(BF16), 1, 0)
    return [jnp.where((before > 0.5) == (slot == 1), onehot, 0.0) for slot in range(2)]


def cross(a, b):
    return (
        a[1] * b[2] - a[2] * b[1],
        a[2] * b[0] - a[0] * b[2],
        a[0] * b[1] - a[1] * b[0],
    )


def dispatch_kernel(anchors, directions, start, cameras, ids, ranks, poses, out, packed):
    bricks = out.shape[0] // 2
    rays = anchors.shape[1]
    spread, own = spread_of(rays)
    id_row = segment_row(ids, spread, own)
    picked = (iota((poses.shape[1], rays), 0) == cameras[...]).astype(F32)
    pose = with_onehot(poses[...], picked, 1, 0)
    turn = [pose[i : i + 1] for i in range(3)]
    anchor = [anchors[i : i + 1, :] for i in range(3)]
    direction = [directions[i : i + 1, :] for i in range(3)]
    turned = cross(turn, anchor)
    bent = cross(turn, direction)
    for i in range(3):
        packed[i : i + 1, :] = anchor[i] + turned[i] + pose[3 + i : 4 + i]
        packed[3 + i : 4 + i, :] = direction[i] + bent[i]
    packed[6:9, :] = anchors[...]
    packed[9:12, :] = directions[...]
    packed[12:13, :] = start[...]
    packed[13:14, :] = cameras[...].astype(F32)
    packed[14:16, :] = jnp.zeros((2, rays), F32)
    rank_row = segment_row(ranks, spread, own)
    values = with_onehot(packed[...], spread, 1, 0)
    values = values + jnp.where(iota((16, 1), 0) == 12, rank_row * (S * STEP), 0.0)
    for slot, taken in enumerate(route_of(id_row, bricks)):
        rows = select_rows(taken, values, 1, 1)
        both = jnp.concatenate([rows, jnp.zeros((bricks, LANES - 16), F32)], axis=1)
        out[pl.ds(slot, bricks, stride=2), :] = both


def dispatch(anchors, directions, start, cameras, ids, ranks, poses, bricks):
    return pl.pallas_call(
        dispatch_kernel,
        out_shape=jax.ShapeDtypeStruct((2 * bricks, LANES), F32),
        scratch_shapes=[pltpu.VMEM((16, anchors.shape[1]), F32)],
        compiler_params=grant(2),
        name="dispatch",
    )(*map(far, (anchors, directions, start, cameras, ids, ranks, poses)))


def ray_rows(received, sources):
    return jnp.concatenate(
        [received[pl.ds(slot, sources, stride=2), :].T[0:16] for slot in range(2)], axis=1
    )


def sample_rows(rows):
    distance = [rows[12:13] + (s + 0.5) * STEP for s in range(S)]
    return [
        jnp.concatenate(
            [rows[i : i + 1] + distance[s] * rows[3 + i : 4 + i] for s in range(S)], axis=1
        )
        for i in range(3)
    ]


def factors(coordinate):
    count = coordinate.shape[1]
    scaled = coordinate * CELLS
    floor_c = jnp.floor(scaled)
    fraction = scaled - floor_c
    weight = fraction * fraction * (3.0 - 2.0 * fraction)
    slope = (6.0 * CELLS) * fraction * (1.0 - fraction)
    low = lax.bitwise_and(floor_c.astype(jnp.int32), CELLS - 1)
    high = lax.bitwise_and(low + 1, CELLS - 1)
    cell = iota((CELLS, count), 0)
    at_low = cell == low
    at_high = cell == high
    value = jnp.where(at_low, 1.0 - weight, 0.0) + jnp.where(at_high, weight, 0.0)
    change = jnp.where(at_high, slope, 0.0) - jnp.where(at_low, slope, 0.0)
    return value, change


BLOCK = 1024
TILE = 256


def plane_axes(step):
    plane = step // (CELLS * CELLS // BLOCK)
    first = plane // 2
    second = min(plane + 1, 2) if isinstance(step, int) else jnp.minimum(plane + 1, 2)
    start = (step % (CELLS * CELLS // BLOCK)) * (BLOCK // CELLS)
    return first * CELLS + start, second * CELLS, first, second


def table_tile(rows_ref, row_base, part, columns, lane):
    pieces = []
    for i in range(TILE // CELLS):
        row = rows_ref[pl.ds(row_base + part * (TILE // CELLS) + i, 1), lane : lane + TILE]
        pieces.append((row * columns).astype(BF16))
    return jnp.concatenate(pieces, axis=0)


IN_HBM = pl.BlockSpec(memory_space=pltpu.HBM)
IN_VMEM = pl.BlockSpec(memory_space=pltpu.VMEM)


def shapes(*arrays):
    return [jax.ShapeDtypeStruct(x.shape, x.dtype) for x in arrays]


def fetch(sources, places, sems, first=0):
    copies = [
        pltpu.make_async_copy(source, place, sems.at[first + i])
        for i, (source, place) in enumerate(zip(sources, places))
    ]
    for copy in copies:
        copy.start()
    return copies


def plane_copies(planes, held, sems, first_step, last_step):
    def copy(step):
        start = pl.multiple_of(step * BLOCK, BLOCK)
        local = pl.multiple_of((step - first_step) * BLOCK, BLOCK)
        return pltpu.make_async_copy(
            planes.at[pl.ds(start, BLOCK), :], held.at[pl.ds(local, BLOCK), :], sems.at[step - first_step]
        )

    for step in range(first_step, last_step):
        copy(step).start()
    return copy


def prepare_kernel(
    planes, first_h, hidden_h, feature_h, density_h, ids_h,
    turned, first_t, hidden_t, feature_t, density_w, first_oh, hidden_oh, feature_oh, route_h,
    held, first_w, hidden_w, feature_w, ids, first_o, hidden_o, feature_o, route, plane_sems, in_sems, out_sems,
):
    steps = planes.shape[0] // BLOCK
    arriving = fetch(
        (ids_h, first_h, hidden_h, feature_h, density_h), (ids, first_w, hidden_w, feature_w, density_w), in_sems
    )
    plane_copy = plane_copies(planes, held, plane_sems, 0, steps)
    for copy in arriving:
        copy.wait()
    for source, plain, flipped in (
        (first_w, first_o, first_t),
        (hidden_w, hidden_o, hidden_t),
        (feature_w, feature_o, feature_t),
    ):
        plain[...] = source[...].astype(BF16)
        flipped[...] = source[...].T.astype(BF16)
    bricks = route.shape[0] // 4
    spread, own = spread_of(ids.shape[1])
    for slot, taken in enumerate(route_of(segment_row(ids, spread, own), bricks)):
        route[slot * bricks : (slot + 1) * bricks, :] = taken.astype(BF16)
        route[(2 + slot) * bricks : (3 + slot) * bricks, :] = taken.T.astype(BF16)
    leaving = fetch((first_o, hidden_o, feature_o, route), (first_oh, hidden_oh, feature_oh, route_h), out_sems)

    @pl.loop(0, steps)
    def _(step):
        plane_copy(step).wait()
        span = pl.ds(pl.multiple_of(step * BLOCK, BLOCK), BLOCK)
        turned[:, span] = held[span, :].T.astype(BF16)

    for copy in leaving:
        copy.wait()


def prepare(planes, first_w, hidden_w, feature_w, density_w, ids, bricks):
    cells, channels = planes.shape
    flips = [jax.ShapeDtypeStruct(w.shape[::-1], BF16) for w in (first_w, hidden_w, feature_w)]
    plains = [pltpu.HBM(w.shape, BF16) for w in (first_w, hidden_w, feature_w)]
    return pl.pallas_call(
        prepare_kernel,
        in_specs=[IN_HBM] * 6,
        out_specs=[IN_VMEM] * 5 + [IN_HBM] * 4,
        out_shape=[jax.ShapeDtypeStruct((channels, cells), BF16)]
        + flips
        + shapes(density_w)
        + plains
        + [pltpu.HBM((4 * bricks, ids.shape[1] * K), BF16)],
        scratch_shapes=[pltpu.VMEM((cells, channels), F32)]
        + [pltpu.VMEM(x.shape, x.dtype) for x in (first_w, hidden_w, feature_w, ids)]
        + [pltpu.VMEM(w.shape, BF16) for w in (first_w, hidden_w, feature_w)]
        + [
            pltpu.VMEM((4 * bricks, ids.shape[1] * K), BF16),
            pltpu.SemaphoreType.DMA((cells // BLOCK,)),
            pltpu.SemaphoreType.DMA((5,)),
            pltpu.SemaphoreType.DMA((4,)),
        ],
        compiler_params=grant(16),
        cost_estimate=price(0, 10 * 2**20),
        name="prepare",
    )(*map(far, (planes, first_w, hidden_w, feature_w, density_w, ids)))


def forward_kernel(
    received, turned, first_t, hidden_t, feature_t, density_w,
    out_h, rows_h, points_h, feats_h, v1_h, v2_h, colors_h, turned_h,
    out, rows_v, points_v, feats_v, v1_v, v2_v, colors_v,
    factor, total, out_sems,
):
    sources = received.shape[0] // 2
    slots = 2 * sources
    count = slots * S
    steps = turned.shape[1] // BLOCK
    leaving = fetch((turned,), (turned_h,), out_sems, 7)
    rows = ray_rows(received, sources)
    rows_v[...] = rows
    points = sample_rows(rows)
    for axis, coordinate in enumerate(points):
        factor[axis * CELLS : (axis + 1) * CELLS, :] = factors(coordinate)[0]
        points_v[axis : axis + 1, :] = coordinate
    points_v[3:8, :] = jnp.zeros((5, count), F32)
    leaving += fetch((rows_v, points_v), (rows_h, points_h), out_sems)
    total[...] = jnp.zeros_like(total)

    for step in range(steps):
        row_base, col_base, _, _ = plane_axes(step)
        for lane in range(0, count, TILE):
            columns = factor[col_base : col_base + CELLS, lane : lane + TILE]
            acc = total[:, lane : lane + TILE]
            for part in range(BLOCK // TILE):
                tile = table_tile(factor, row_base, part, columns, lane)
                start = step * BLOCK + part * TILE
                acc = acc + contract(turned[:, start : start + TILE], tile, 1, 0)
            total[:, lane : lane + TILE] = acc

    feats = total[...].astype(BF16)
    feats_v[...] = feats
    v1 = contract(first_t[...], feats, 1, 0)
    v1_v[...] = v1
    leaving += fetch((feats_v, v1_v), (feats_h, v1_h), out_sems, 2)
    h1 = (v1 * jax.nn.sigmoid(v1)).astype(BF16)
    v2 = contract(hidden_t[...], h1, 1, 0)
    v2_v[...] = v2
    leaving += fetch((v2_v,), (v2_h,), out_sems, 4)
    h2 = (v2 * jax.nn.sigmoid(v2)).astype(BF16)
    colors = jnp.tanh(contract(feature_t[...], h2, 1, 0))
    colors_v[0:LANES, :] = colors
    raw = contract(density_w[...].astype(BF16), h2, 1, 0)
    colors_v[LANES : LANES + 8, :] = jnp.broadcast_to(raw, (8, count))
    leaving += fetch((colors_v,), (colors_h,), out_sems, 5)
    depth = (jnp.maximum(raw, 0.0) + jnp.log1p(jnp.exp(-jnp.abs(raw)))) * STEP
    seg = jnp.zeros((LANES, slots), F32)
    front = jnp.zeros((1, slots), F32)
    for s in range(S):
        e = depth[:, s * slots : (s + 1) * slots]
        weight = jnp.exp(-front) * (1.0 - jnp.exp(-e))
        seg = seg + weight * colors[:, s * slots : (s + 1) * slots]
        front = front + e
    through = jnp.exp(-front)
    out[pl.ds(0, sources, stride=3), :] = seg[:, 0:sources].T
    out[pl.ds(1, sources, stride=3), :] = seg[:, sources:slots].T
    sub = iota((LANES, sources), 0)
    both = jnp.where(
        sub == 0, through[:, 0:sources], jnp.where(sub == 1, through[:, sources:slots], 0.0)
    )
    out[pl.ds(2, sources, stride=3), :] = both.T
    leaving += fetch((out,), (out_h,), out_sems, 6)
    for copy in leaving:
        copy.wait()


def forward(received, turned, first_t, hidden_t, feature_t, density_w):
    sources = received.shape[0] // 2
    slots = 2 * sources
    count = slots * S
    channels, cells = turned.shape
    hidden = first_t.shape[0]
    saved = [
        ((3 * sources, LANES), F32),
        ((16, slots), F32),
        ((8, count), F32),
        ((channels, count), BF16),
        ((hidden, count), F32),
        ((hidden, count), F32),
        ((channels + 8, count), F32),
    ]
    return pl.pallas_call(
        forward_kernel,
        in_specs=[IN_VMEM] * 6,
        out_specs=[IN_HBM] * (len(saved) + 1),
        out_shape=[pltpu.HBM(shape, kind) for shape, kind in saved + [(turned.shape, BF16)]],
        scratch_shapes=[pltpu.VMEM(shape, kind) for shape, kind in saved]
        + [
            pltpu.VMEM((3 * CELLS, count), F32),
            pltpu.VMEM((channels, count), F32),
            pltpu.SemaphoreType.DMA((len(saved) + 1,)),
        ],
        compiler_params=grant(16),
        cost_estimate=price(2 * cells * count * channels, 8 * 2**20),
        name="forward",
    )(received, turned, first_t, hidden_t, feature_t, density_w)


def slopes(points, planes_t, first_step, last_step, carried, begun=None):
    count = points.shape[1]
    channels = planes_t.shape[0]
    steps = last_step - first_step
    moved = len(carried)
    ending = begun is not None
    ins = list(carried) + ([begun] if ending else [])

    def slope_kernel(points_h, planes_h, *refs):
        given, refs = refs[: len(ins)], refs[len(ins) :]
        out, brought, refs = refs[0], refs[1 : 1 + moved], refs[1 + moved :]
        turned, points, factor, slope, total, plane_sems, in_sems = refs[:7]
        if ending:
            total = out
        else:
            rounded, out_sems = refs[7:]
        arriving = fetch((points_h,), (points,), in_sems)
        blocks = [
            pltpu.make_async_copy(
                planes_h.at[:, (first_step + step) * BLOCK : (first_step + step + 1) * BLOCK],
                turned.at[:, step * BLOCK : (step + 1) * BLOCK],
                plane_sems.at[step],
            )
            for step in range(steps)
        ]
        for copy in blocks:
            copy.start()
        arriving += fetch(given, brought + (refs[7:] if ending else ()), in_sems, 1)
        total[...] = jnp.zeros_like(total)
        arriving[0].wait()
        for axis in range(3):
            span = slice(axis * CELLS, (axis + 1) * CELLS)
            factor[span, :], slope[span, :] = factors(points[axis : axis + 1, :])

        leaving = []
        for step in range(steps):
            blocks[step].wait()
            row_base, col_base, first, second = plane_axes(first_step + step)
            for rows_ref, cols_ref, axis in ((slope, factor, first), (factor, slope, second)):
                rows = slice(axis * LANES, (axis + 1) * LANES)
                for lane in range(0, count, TILE):
                    here = slice(lane, lane + TILE)
                    columns = cols_ref[col_base : col_base + CELLS, here]
                    acc = total[rows, here]
                    for part in range(BLOCK // TILE):
                        tile = table_tile(rows_ref, row_base, part, columns, lane)
                        start = step * BLOCK + part * TILE
                        acc = acc + contract(turned[:, start : start + TILE], tile, 1, 0)
                    total[rows, here] = acc
        if ending:
            for copy in arriving[1:]:
                copy.wait()
            out[...] = out[...] + refs[7][...].astype(F32)
        else:
            for axis in range(3):
                rows = slice(axis * LANES, (axis + 1) * LANES)
                rounded[rows, :] = total[rows, :].astype(BF16)
                copy = pltpu.make_async_copy(rounded.at[rows, :], out.at[rows, :], out_sems.at[axis])
                copy.start()
                leaving.append(copy)
            for copy in arriving[1:] + leaving:
                copy.wait()

    shape = (3 * channels, count)
    return pl.pallas_call(
        slope_kernel,
        in_specs=[IN_HBM] * (2 + len(ins)),
        out_specs=[IN_VMEM if ending else IN_HBM] + [IN_VMEM] * moved,
        out_shape=[jax.ShapeDtypeStruct(shape, F32) if ending else pltpu.HBM(shape, BF16)] + shapes(*carried),
        scratch_shapes=[
            pltpu.VMEM((channels, steps * BLOCK), BF16),
            pltpu.VMEM(points.shape, F32),
            pltpu.VMEM((3 * CELLS, count), F32),
            pltpu.VMEM((3 * CELLS, count), F32),
            pltpu.VMEM((8, 128) if ending else shape, F32),
            pltpu.SemaphoreType.DMA((steps,)),
            pltpu.SemaphoreType.DMA((1 + len(ins),)),
        ]
        + [pltpu.VMEM(shape, BF16)]
        + ([] if ending else [pltpu.SemaphoreType.DMA((3,))]),
        compiler_params=grant(16),
        cost_estimate=price(4 * steps * BLOCK * count * channels, 6 * 2**20),
        name="slopes",
    )(far(points), far(planes_t), *map(far, ins))


def rays_kernel(home, route, ranks, targets, ray_h, back_h, ray_out, back, grads, out_sems):
    bricks = home.shape[0] // 3
    rays = targets.shape[0]
    slot = [route[(2 + c) * bricks : (3 + c) * bricks, :] for c in range(2)]
    seg = select_rows(slot[0], home[pl.ds(0, bricks, stride=3), :], 1, 0) + select_rows(
        slot[1], home[pl.ds(1, bricks, stride=3), :], 1, 0
    )
    lane = iota((1, LANES), 1)
    through = home[pl.ds(2, bricks, stride=3), :]
    passing = jnp.sum(
        select_rows(slot[0], jnp.where(lane == 0, through, 0.0), 1, 0)
        + select_rows(slot[1], jnp.where(lane == 1, through, 0.0), 1, 0),
        axis=1,
        keepdims=True,
    )
    feature = [seg[k * rays : (k + 1) * rays] for k in range(K)]
    pass_k = [passing[k * rays : (k + 1) * rays] for k in range(K)]
    rank_cols = contract(eye(rays), ranks[...].astype(F32), 1, 1, EXACT)
    rank = [rank_cols[:, k : k + 1] for k in range(K)]
    ones = jnp.ones((rays, 1), F32)

    def seen(k, skip=None):
        product = ones
        for other in range(K):
            if other != k and other != skip:
                product = product * jnp.where(rank[other] < rank[k], pass_k[other], 1.0)
        return product

    transmit = [seen(k) for k in range(K)]
    ray = jnp.zeros_like(feature[0])
    for k in range(K):
        ray = ray + transmit[k] * feature[k]
    ray_out[...] = ray
    leaving = fetch((ray_out,), (ray_h,), out_sems)
    grad = ray - targets[...]
    pull = [jnp.sum(grad * feature[k], axis=1, keepdims=True) for k in range(K)]
    for k in range(K):
        grads[k * rays : (k + 1) * rays, 0:LANES] = transmit[k] * grad
        pass_grad = jnp.zeros((rays, 1), F32)
        for behind in range(K):
            if behind != k:
                pass_grad = pass_grad + jnp.where(
                    rank[k] < rank[behind], pull[behind] * seen(behind, k), 0.0
                )
        grads[k * rays : (k + 1) * rays, LANES : 2 * LANES] = jnp.broadcast_to(
            pass_grad, (rays, LANES)
        )
    spread = None
    for c in range(2):
        both = select_rows(route[c * bricks : (c + 1) * bricks, :], grads[...], 1, 0)
        back[pl.ds(c, bricks, stride=3), :] = both[:, 0:LANES]
        own = jnp.where(lane == c, both[:, LANES : 2 * LANES], 0.0)
        spread = own if spread is None else spread + own
    back[pl.ds(2, bricks, stride=3), :] = spread
    leaving += fetch((back,), (back_h,), out_sems, 1)
    for copy in leaving:
        copy.wait()


def rays_step(home, route, ranks, targets):
    return pl.pallas_call(
        rays_kernel,
        out_specs=[IN_HBM] * 2,
        out_shape=(pltpu.HBM(targets.shape, F32), pltpu.HBM(home.shape, F32)),
        scratch_shapes=[
            pltpu.VMEM(targets.shape, F32),
            pltpu.VMEM(home.shape, F32),
            pltpu.VMEM((route.shape[1], 2 * LANES), F32),
            pltpu.SemaphoreType.DMA((2,)),
        ],
        compiler_params=grant(4),
        name="rays",
    )(home, route, ranks, targets)


def backward_kernel(
    cot, slope_ref, colors_ref, v2_ref, feature_w, density_h, v1_h, hidden_h, first_h, rows_h,
    pose_gh, feat_cot_h, color_gh, h2_gh, raw_gh, v2_gh, h1_gh, v1_gh,
    density_w, v1_ref, hidden_w, first_w, rows_ref,
    feat_cot, color_cot, h2_v, raw_v, v2_cot_v, h1_v, v1_cot_v, pair, pose_g, in_sems, out_sems,
):
    arriving = fetch(
        (density_h, v1_h, hidden_h, first_h, rows_h),
        (density_w, v1_ref, hidden_w, first_w, rows_ref),
        in_sems,
    )
    sources = cot.shape[0] // 3
    slots = 2 * sources
    seg_cot = jnp.concatenate(
        [cot[pl.ds(slot, sources, stride=3), :].T for slot in range(2)], axis=1
    )
    turned = cot[pl.ds(2, sources, stride=3), :].T
    pass_cot = jnp.concatenate([turned[0:1], turned[1:2]], axis=1)
    raw = colors_ref[LANES : LANES + 1, :]
    depth = (jnp.maximum(raw, 0.0) + jnp.log1p(jnp.exp(-jnp.abs(raw)))) * STEP
    front = jnp.zeros((1, slots), F32)
    weights, kept, pulls = [], [], []
    for s in range(S):
        span = slice(s * slots, (s + 1) * slots)
        e = depth[:, span]
        reach = jnp.exp(-front)
        weight = reach * (1.0 - jnp.exp(-e))
        colors = colors_ref[0:LANES, span]
        pulls.append(jnp.sum(colors * seg_cot, axis=0, keepdims=True))
        color_cot[:, span] = (weight * seg_cot * (1.0 - colors * colors)).astype(BF16)
        weights.append(weight)
        kept.append(reach * jnp.exp(-e))
        front = front + e
    behind = pass_cot * jnp.exp(-front)
    depth_cot = [None] * S
    for s in reversed(range(S)):
        depth_cot[s] = pulls[s] * kept[s] - behind
        behind = behind + pulls[s] * weights[s]
    raw_cot = (jnp.concatenate(depth_cot, axis=1) * STEP * jax.nn.sigmoid(raw)).astype(BF16)

    v2 = v2_ref[...]
    gate2 = jax.nn.sigmoid(v2)
    h2 = (v2 * gate2).astype(BF16)
    color_c = color_cot[...]
    h2_v[...] = h2
    leaving = fetch((color_cot, h2_v), (color_gh, h2_gh), out_sems)
    arriving[0].wait()
    wide = jnp.where(iota((8, 1), 0) == 0, density_w[...].astype(F32), 0.0).astype(BF16)
    wide_cot = jnp.where(iota((8, 1), 0) == 0, raw_cot.astype(F32), 0.0).astype(BF16)
    raw_v[...] = wide_cot
    h2_cot = (
        contract(feature_w[...], color_c, 1, 0) + contract(wide.T, wide_cot, 1, 0)
    ).astype(BF16).astype(F32)
    v2_cot = (h2_cot * gate2 * (1.0 + v2 * (1.0 - gate2))).astype(BF16)
    for copy in arriving[1:]:
        copy.wait()
    v1 = v1_ref[...]
    gate1 = jax.nn.sigmoid(v1)
    h1 = (v1 * gate1).astype(BF16)
    h1_v[...] = h1
    v2_cot_v[...] = v2_cot
    leaving += fetch((raw_v, v2_cot_v, h1_v), (raw_gh, v2_gh, h1_gh), out_sems, 2)
    h1_cot = contract(hidden_w[...], v2_cot, 1, 0).astype(BF16).astype(F32)
    v1_cot = (h1_cot * gate1 * (1.0 + v1 * (1.0 - gate1))).astype(BF16)
    v1_cot_v[...] = v1_cot
    leaving += fetch((v1_cot_v,), (v1_gh,), out_sems, 5)
    f_cot = contract(first_w[...], v1_cot, 1, 0).astype(BF16).astype(F32)
    feat_cot[...] = f_cot.T.astype(BF16)
    leaving += fetch((feat_cot,), (feat_cot_h,), out_sems, 6)

    pull = [
        jnp.sum(slope_ref[a * LANES : (a + 1) * LANES, :] * f_cot, axis=0, keepdims=True)
        for a in range(3)
    ]
    rows = rows_ref[...]
    shift = [jnp.zeros((1, slots), F32)] * 3
    turn = [jnp.zeros((1, slots), F32)] * 3
    for s in range(S):
        distance = rows[12:13] + (s + 0.5) * STEP
        place = [rows[6 + i : 7 + i] + distance * rows[9 + i : 10 + i] for i in range(3)]
        part = [pull[a][:, s * slots : (s + 1) * slots] for a in range(3)]
        twist = cross(place, part)
        for a in range(3):
            shift[a] = shift[a] + part[a]
            turn[a] = turn[a] + twist[a]
    sub = iota((8, slots), 0)
    grads = jnp.zeros((8, slots), F32)
    for a in range(3):
        grads = jnp.where(sub == a, turn[a], grads)
        grads = jnp.where(sub == 3 + a, shift[a], grads)
    cams = 2 * LANES
    picked = (iota((cams, slots), 0) == rows[13:14].astype(jnp.int32)).astype(F32)
    pose = with_onehot(grads, picked, 1, 1)
    for copy in range(2):
        for half in range(2):
            start = copy * 12 + half * 6
            pair[start : start + 6, :] = pose[0:6, half * LANES : (half + 1) * LANES]
    two = pair[...]
    for copy in range(pose_g.shape[0] // 24):
        pose_g[copy * 24 : (copy + 1) * 24, :] = two
    leaving += fetch((pose_g,), (pose_gh,), out_sems, 7)
    for copy in leaving:
        copy.wait()


def backward(cot, near, distant, copies):
    first_w = distant[3]
    channels, hidden = first_w.shape
    count = near[0].shape[1]
    outs = [
        ((count, channels), BF16),
        ((channels, count), BF16),
        ((hidden, count), BF16),
        ((8, count), BF16),
        ((hidden, count), BF16),
        ((hidden, count), BF16),
        ((hidden, count), BF16),
    ]
    return pl.pallas_call(
        backward_kernel,
        in_specs=[IN_VMEM] * (len(near) + 1) + [IN_HBM] * len(distant),
        out_specs=[IN_HBM] * (1 + len(outs)),
        out_shape=[pltpu.HBM((12 * copies, LANES), F32)] + [pltpu.HBM(shape, kind) for shape, kind in outs],
        scratch_shapes=[pltpu.VMEM(x.shape, x.dtype) for x in distant]
        + [pltpu.VMEM(shape, kind) for shape, kind in outs]
        + [
            pltpu.VMEM((24, LANES), F32),
            pltpu.VMEM((12 * copies, LANES), F32),
            pltpu.SemaphoreType.DMA((len(distant),)),
            pltpu.SemaphoreType.DMA((1 + len(outs),)),
        ],
        compiler_params=grant(16),
        name="backward",
    )(cot, *near, *map(far, distant))


def gradient_kernel(
    points_h, cot_h, color_h, h2_h, raw_h, v2_h, h1_h, v1_h, feats_h,
    planes_gh, first_gh, hidden_gh, feature_gh, density_gh,
    points, cot, color_c, h2, raw_c, v2_cot, h1, v1_cot, feats,
    planes_g, first_g, hidden_g, feature_g, density_g,
    factor, in_sems, plane_sems, out_sems,
):
    count = points.shape[1]
    arriving = fetch(
        (points_h, cot_h, color_h, h2_h, raw_h, v2_h, h1_h, v1_h, feats_h),
        (points, cot, color_c, h2, raw_c, v2_cot, h1, v1_cot, feats),
        in_sems,
    )
    arriving[0].wait()
    for axis in range(3):
        factor[axis * CELLS : (axis + 1) * CELLS, :] = factors(points[axis : axis + 1, :])[0]
    arriving[1].wait()
    blocks = planes_g.shape[0] // BLOCK
    leaving = []
    for block in range(blocks):
        row_base, col_base, _, _ = plane_axes(block)
        for part in range(BLOCK // TILE):
            acc = jnp.zeros((TILE, cot.shape[1]), F32)
            for lane in range(0, count, TILE):
                columns = factor[col_base : col_base + CELLS, lane : lane + TILE]
                tile = table_tile(factor, row_base, part, columns, lane)
                acc = acc + contract(tile, cot[lane : lane + TILE, :], 1, 0)
            start = block * BLOCK + part * TILE
            planes_g[start : start + TILE, :] = acc
        rows = slice(block * BLOCK, (block + 1) * BLOCK)
        copy = pltpu.make_async_copy(planes_g.at[rows, :], planes_gh.at[rows, :], plane_sems.at[block])
        copy.start()
        leaving.append(copy)
        if block == blocks // 2:
            for arrival in arriving[2:]:
                arrival.wait()
            first_g[...] = contract(feats[...], v1_cot[...], 1, 1).astype(BF16).astype(F32)
            hidden_g[...] = contract(h1[...], v2_cot[...], 1, 1).astype(BF16).astype(F32)
            feature_g[...] = contract(h2[...], color_c[...], 1, 1).astype(BF16).astype(F32)
            density_g[...] = contract(raw_c[...], h2[...], 1, 1)[0:1].astype(BF16).astype(F32)
            leaving += fetch(
                (first_g, hidden_g, feature_g, density_g), (first_gh, hidden_gh, feature_gh, density_gh), out_sems
            )
    for copy in leaving:
        copy.wait()


def gradients(points, cots, feats, cells):
    count = points.shape[1]
    cot, color_c, h2 = cots[:3]
    channels, hidden = feats.shape[0], h2.shape[0]
    ins = [points, *cots, feats]
    outs = [(cells, channels), (channels, hidden), (hidden, hidden), (hidden, channels), (1, hidden)]
    return pl.pallas_call(
        gradient_kernel,
        in_specs=[IN_HBM] * len(ins),
        out_specs=[IN_HBM] * len(outs),
        out_shape=[pltpu.HBM(shape, F32) for shape in outs],
        scratch_shapes=[pltpu.VMEM(x.shape, x.dtype) for x in ins]
        + [pltpu.VMEM(shape, F32) for shape in outs]
        + [
            pltpu.VMEM((3 * CELLS, count), F32),
            pltpu.SemaphoreType.DMA((len(ins),)),
            pltpu.SemaphoreType.DMA((cells // BLOCK,)),
            pltpu.SemaphoreType.DMA((4,)),
        ],
        compiler_params=grant(24),
        cost_estimate=price(2 * cells * count * channels, cells * channels * 4),
        name="gradients",
    )(*map(far, ins))


def exchange(rows, peers):
    wide = rows.reshape(peers, 1, rows.size // peers)
    moved = lax.all_to_all(wide, AXES, split_axis=0, concat_axis=0, tiled=True)
    return moved.reshape(rows.shape)


def add_kernel(parts, out):
    total = parts[0:24, :]
    for source in range(1, parts.shape[0] // 24):
        total = total + parts[source * 24 : (source + 1) * 24, :]
    total = total[0:12] + total[12:24]
    out[:, 0:LANES] = total[0:6]
    out[:, LANES : 2 * LANES] = total[6:12]


def add(parts, shape):
    return pl.pallas_call(
        add_kernel, out_shape=pltpu.HBM(shape, F32), compiler_params=grant(2), name="add"
    )(parts)


def per_device(
    anchors, directions, ray_start, camera_ids, brick_ids, brick_rank, targets,
    planes, first_weight, hidden_weight, feature_weight, density_weight, poses,
):
    bricks = lax.axis_size(AXES)
    cells = planes.shape[1]
    steps = cells // BLOCK
    ids, ranks = brick_ids.T, brick_rank.T
    outgoing = dispatch(
        anchors, directions, ray_start[None], camera_ids[None], ids, ranks, poses, bricks
    )
    received = exchange(outgoing, bricks)
    turned, first_t, hidden_t, feature_t, density_o, first_o, hidden_o, feature_o, route = prepare(
        planes[0], first_weight[0], hidden_weight[0, 0], feature_weight[0], density_weight, ids, bricks
    )
    sent, rows, points, feats, v1, v2, colors, turned_far = forward(
        received, turned, first_t, hidden_t, feature_t, density_o
    )
    home = exchange(sent, bricks)
    begun, *ray_data = slopes(points, turned_far, 0, steps // 2, [route, ranks, targets])
    ray_feature, back = rays_step(home, *ray_data)
    cot = exchange(back, bricks)
    later_points, back = lax.optimization_barrier((points, back))
    near = slopes(
        later_points, turned_far, steps // 2, steps, [colors, v2, feature_o], begun
    )
    distant = [density_weight, v1, hidden_o, first_o, rows]
    pose_part, *cots = backward(cot, near, distant, bricks)
    pose_grad = add(exchange(pose_part, bricks), poses.shape)
    plane_grad, first_g, hidden_g, feature_g, density_g = gradients(points, cots, feats, cells)
    return (
        ray_feature,
        plane_grad[None],
        first_g[None],
        hidden_g[None, None],
        feature_g[None],
        density_g,
        pose_grad,
    )


def solution(mesh):
    rays = P(AXES)
    in_specs = (
        P(None, AXES), P(None, AXES), rays, rays, P(AXES, None), P(AXES, None), P(AXES, None),
        P(AXES, None, None), P(AXES, None, None), P(AXES, None, None, None), P(AXES, None, None),
        P(AXES, None), P(),
    )
    out_specs = (
        P(AXES, None), P(AXES, None, None), P(AXES, None, None), P(AXES, None, None, None),
        P(AXES, None, None), P(AXES, None), P(),
    )
    return jax.shard_map(
        per_device, mesh=mesh, in_specs=in_specs, out_specs=out_specs, check_vma=False
    )
```
